32 devices in a mesh: groups: 2 (over y), leaf: 4 (over z), vec: 2 (over x), lvl: 2 (over core).
Axes of the slice: x: 2, y: 2, z: 4, core: 2. Of those that a mesh axis runs over, the one named last changes fastest.
Arguments:
- adjoint_in: bfloat16 [128, 8192], P('groups', 'leaf'), parts along dimension 0, may hold values from -6 to 6
- row_basis: bfloat16 [64, 64, 256], P(('groups', 'leaf')), parts along dimension 0, may hold values from -0.375 to 0.375
- col_basis: bfloat16 [64, 64, 256], P(('groups', 'leaf')), parts along dimension 0, may hold values from -0.75 to 0.75
- row_transfer: bfloat16 [64, 64, 64], P(('groups', 'leaf')), parts along dimension 0, may hold values from -0.75 to 0.75
- col_transfer: bfloat16 [64, 64, 64], P(('groups', 'leaf')), parts along dimension 0, may hold values from -0.75 to 0.75
- parents: int32 [64], P(('groups', 'leaf')), parts along dimension 0, may hold values from 0 to 7, never falling along the last dimension, each value on 1 to 8 neighbouring positions
- far_sources: int32 [64, 64], P(('groups', 'leaf')), parts along dimension 0, may hold values from 0 to 31
- far_blocks: bfloat16 [64, 64, 64, 64], P(('groups', 'leaf'), ('vec', 'lvl')), parts along dimension 0, may hold values from -0.09375 to 0.09375
- coarse_sources: int32 [16, 32], P(('groups', 'leaf')), parts along dimension 0, may hold values from 0 to 7
- coarse_blocks: bfloat16 [16, 32, 64, 64], P(('groups', 'leaf'), ('vec', 'lvl')), parts along dimension 0, may hold values from -0.0625 to 0.0625
- near_sources: int32 [64, 16], P(('groups', 'leaf')), parts along dimension 0, may hold values from 0 to 31, as said below
- near_blocks: bfloat16 [64, 16, 256, 256], P(('groups', 'leaf'), ('vec', 'lvl')), parts along dimension 0, may hold values from -0.09375 to 0.09375
Outputs:
- adjoint_out: bfloat16 [128, 8192], P(('groups', 'vec', 'lvl'), 'leaf'), parts along dimension 0
The draws below stay inside these ranges and needn't reach their ends.
There are 2 independent parts, one for each index of `groups`. The reference program is written for one: setup_inputs(seed, part) draws one part's arguments, and reference() takes and returns one part's arrays. A program takes and returns all parts, laid end to end along the dimension named above; each array names one. Nothing has to cross between parts.
Inputs may be any that keep to these rules, and one draw needn't show every extreme that they name: `parents`: never falling along the leaves; every cluster has 1 to 8 leaves, and some cluster exactly 8. `near_sources`: every entry names a leaf at most 2 leaves away from its own leaf along the curve; every leaf's list names the leaf 2 before it and the leaf 2 after it, where these exist.
All inputs are finite; a program needn't handle non-finite values.
Results may differ from the reference program's by a relative error of at most 0.0061.
Values may be sent and summed in bfloat16 or wider, within the bound.
No kernel may reach another device: no remote copies, remote signals or barrier semaphores. Data moves between devices by JAX's collectives and lax.ppermute only.
A program may use at most 64 MiB of HBM per device.

```python
import math
import jax
import jax.numpy as jnp
import numpy as np
from jax import lax

K = 64
P_SIZE = 256
R = 64
FAR = 64
CFAR = 32
NEAR = 16
REACH = 2
LEAVES = 32
CLUST = 8
PANELS = 8192


def draw_near_sources(key, part):
    offsets = jax.random.randint(jax.random.fold_in(key, 11), (LEAVES, NEAR), -REACH, REACH + 1)
    slot_before = jax.random.randint(jax.random.fold_in(key, 12), (LEAVES, 1), 0, NEAR)
    stride = jax.random.randint(jax.random.fold_in(key, 13), (LEAVES, 1), 1, NEAR)
    slot_after = (slot_before + stride) % NEAR
    column = jnp.arange(NEAR, dtype=jnp.int32)[None, :]
    offsets = jnp.where(column == slot_before, -REACH, offsets)
    offsets = jnp.where(column == slot_after, REACH, offsets)
    leaf_ids = jnp.arange(LEAVES, dtype=jnp.int32)[:, None]
    return jnp.clip(leaf_ids + offsets, 0, LEAVES - 1).astype(jnp.int32)


def set_ends(array, key, least, top_value):
    longest = array.shape.index(max(array.shape))
    spots = []
    for shift in (0, 1):
        where = [jax.random.randint(jax.random.fold_in(key, axis), (), 0, length) for axis, length in enumerate(array.shape)]
        where[longest] = (where[longest] + shift) % array.shape[longest]
        spots.append(tuple(where))
    return array.at[spots[0]].set(least).at[spots[1]].set(top_value)


def block_scale(stream_key, dims, cuts, low, largest):
    loudness, own = 1.0, jax.random.fold_in(stream_key, 6)
    for position, blocks in cuts:
        draws = jnp.exp(jax.random.uniform(jax.random.fold_in(own, position), (blocks,), jnp.float32, low / len(cuts), largest / len(cuts)))
        loudness = loudness * jnp.repeat(draws, dims[position] // blocks).reshape([-1 if axis == position else 1 for axis in range(len(dims))])
    return loudness


def profile(amount, total, bound, lean):
    loads = [(1 << 20) // math.isqrt(grade ** lean) + 1 for grade in range(2, amount + 1)]
    rest, given = total - bound - (amount - 1), [1] * (amount - 1)
    while rest > 0:
        candidates = [i for i in range(amount - 1) if given[i] < bound]
        pool, left = sum([loads[i] for i in candidates]), rest
        for i in candidates:
            more = min(bound - given[i], max(1, left * loads[i] // pool), rest)
            given[i] = given[i] + more
            rest = rest - more
    return np.array([bound] + given)


def ragged(key, amount, total, bound, lean):
    if amount == 2:
        one = jax.random.randint(key, (), max(1, total - bound), min(bound, total - 1) + 1)
        return jnp.stack([one, total - one])
    sizes = jnp.asarray(profile(amount, total, bound, lean), jnp.int32)
    couples = (amount - 1) // 2
    giver, receiver = sizes[1:1 + 2 * couples:2], sizes[2:2 + 2 * couples:2]
    margin = jnp.minimum(giver - 1, bound - receiver)
    moved = jax.random.randint(jax.random.fold_in(key, 1), (couples,), 0, 1 << 20) % (margin + 1)
    sizes = sizes.at[1:1 + 2 * couples:2].set(giver - moved).at[2:2 + 2 * couples:2].set(receiver + moved)
    return sizes[jax.random.permutation(jax.random.fold_in(key, 2), amount)]


def bell_draw(key, extent, deviation, reach, cuts=(), kind=jnp.bfloat16):
    level = block_scale(key, extent, cuts, -0.22, 0.18) if cuts else 1.0
    values = jax.random.normal(key, extent, jnp.float32) * deviation * level
    return jnp.minimum(jnp.maximum(values, -reach), reach).astype(kind)


def setup_inputs(seed: int = 0, part: int = 0) -> dict:
    streams_of = jax.random.split(jax.random.key(seed), 13)
    part_splits = jax.random.split(jax.random.fold_in(streams_of[12], part), 13)
    adjoint_in = bell_draw(part_splits[0], (K, PANELS), 1.0, 6.0, ((1, 4),))
    row_basis = bell_draw(part_splits[1], (LEAVES, R, P_SIZE), P_SIZE ** -0.5, 0.375, ((0, 4),))
    col_basis = bell_draw(part_splits[2], (LEAVES, R, P_SIZE), R ** -0.5, 0.75, ((0, 4),))
    row_transfer = bell_draw(part_splits[3], (LEAVES, R, R), R ** -0.5, 0.75, ((0, 4),))
    col_transfer = bell_draw(part_splits[4], (LEAVES, R, R), R ** -0.5, 0.75, ((0, 4),))
    parents = jnp.searchsorted(jnp.cumsum(ragged(part_splits[5], CLUST, LEAVES, 8, 1)), jnp.arange(LEAVES), side="right").astype(jnp.int32)
    far_sources = set_ends(jax.random.randint(part_splits[6], (LEAVES, FAR), 0, LEAVES), jax.random.fold_in(part_splits[6], 1), 0, LEAVES - 1).astype(jnp.int32)
    far_blocks = bell_draw(part_splits[7], (LEAVES, FAR, R, R), (R * FAR) ** -0.5, 0.09375, ((0, 4), (1, 4)))
    coarse_sources = set_ends(jax.random.randint(part_splits[8], (CLUST, CFAR), 0, CLUST), jax.random.fold_in(part_splits[8], 1), 0, CLUST - 1).astype(jnp.int32)
    coarse_blocks = bell_draw(part_splits[9], (CLUST, CFAR, R, R), (4 * R * CFAR) ** -0.5, 0.0625, ((0, 4), (1, 4)))
    near_sources = draw_near_sources(jax.random.fold_in(jax.random.fold_in(streams_of[12], part), 71), part)
    near_blocks = bell_draw(part_splits[11], (LEAVES, NEAR, P_SIZE, P_SIZE), (P_SIZE * NEAR) ** -0.5, 0.09375, ((0, 4), (1, 4)))
    return {"adjoint_in": adjoint_in, "row_basis": row_basis, "col_basis": col_basis, "row_transfer": row_transfer, "col_transfer": col_transfer, "parents": parents, "far_sources": far_sources, "far_blocks": far_blocks, "coarse_sources": coarse_sources, "coarse_blocks": coarse_blocks, "near_sources": near_sources, "near_blocks": near_blocks}


def reference(adjoint_in, row_basis, col_basis, row_transfer, col_transfer, parents, far_sources, far_blocks, coarse_sources, coarse_blocks, near_sources, near_blocks):
    single = jnp.float32
    x_blocks = adjoint_in.astype(single).reshape(K, LEAVES, P_SIZE)
    leaf_up = jnp.einsum("klp,lrp->lkr", x_blocks, row_basis.astype(single)).astype(jnp.bfloat16)
    branch = jnp.einsum("lkr,lrc->lkc", leaf_up.astype(single), row_transfer.astype(single))
    cluster_up = jax.ops.segment_sum(branch, parents, num_segments=CLUST).astype(jnp.bfloat16)

    def far_one(inputs):
        sources, blocks = inputs
        rows_in = jnp.take(leaf_up, sources, axis=0).astype(single)
        return jnp.einsum("jkr,jrs->ks", rows_in, blocks.astype(single))

    leaf_down = lax.map(far_one, (far_sources, far_blocks))

    def coarse_one(inputs):
        sources, blocks = inputs
        rows_in = jnp.take(cluster_up, sources, axis=0).astype(single)
        return jnp.einsum("jkr,jrs->ks", rows_in, blocks.astype(single))

    cluster_down = lax.map(coarse_one, (coarse_sources, coarse_blocks)).astype(jnp.bfloat16)
    pushed = jnp.take(cluster_down, parents, axis=0).astype(single)
    leaf_total = (leaf_down + jnp.einsum("lkc,lrc->lkr", pushed, col_transfer.astype(single))).astype(jnp.bfloat16)
    far_out = jnp.einsum("lkr,lrp->klp", leaf_total.astype(single), col_basis.astype(single))

    def near_one(inputs):
        sources, blocks = inputs
        rows_in = jnp.take(x_blocks, sources, axis=1)
        return jnp.einsum("kjp,jpq->kq", rows_in, blocks.astype(single))

    near_out = lax.map(near_one, (near_sources, near_blocks))
    result = far_out + jnp.transpose(near_out, (1, 0, 2))
    return result.reshape(K, LEAVES * P_SIZE).astype(jnp.bfloat16)
```

```python
import functools

import jax
import jax.numpy as jnp
from jax import lax
from jax.experimental import pallas as pl
from jax.experimental.pallas import tpu as pltpu
from jax.sharding import PartitionSpec as P

REACH = 2
BF = jnp.bfloat16
F32 = jnp.float32
VMEM = pl.BlockSpec(memory_space=pltpu.VMEM)
SMEM = pl.BlockSpec(memory_space=pltpu.SMEM)
ANY = pl.BlockSpec(memory_space=pl.ANY)
LIMIT = 48 << 20


def dot(a, b):
    return jnp.dot(a, b, preferred_element_type=F32)


def dot_t(a, b):
    return lax.dot_general(a, b, (((1,), (1,)), ((), ())), preferred_element_type=F32)


def low_half(shape):
    return lax.broadcasted_iota(jnp.int32, shape, len(shape) - 1) < shape[-1] // 2


def swap_halves(x):
    half = x.shape[-1] // 2
    return jnp.concatenate([x[..., half:], x[..., :half]], axis=-1)


def with_halo(block, sides, width):
    for axis, dim in sides:
        count = lax.axis_size(axis)
        forward = [(i, i + 1) for i in range(count - 1)]
        backward = [(target, source) for source, target in forward]
        low = lax.ppermute(
            lax.slice_in_dim(block, block.shape[dim] - width, None, axis=dim), axis, forward
        )
        high = lax.ppermute(lax.slice_in_dim(block, 0, width, axis=dim), axis, backward)
        block = jnp.concatenate([low, block, high], axis=dim)
    return block


def on_device_general(
    adjoint_in,
    row_basis,
    col_basis,
    row_transfer,
    col_transfer,
    parents,
    far_sources,
    far_blocks,
    coarse_sources,
    coarse_blocks,
    near_sources,
    near_blocks,
):
    owner_count = lax.axis_size(("vec", "lvl"))
    owner_index = lax.axis_index(("vec", "lvl"))
    leaf_index = lax.axis_index("leaf")
    leaf_count = lax.axis_size("leaf")
    vector_count = adjoint_in.shape[0]
    leaf_rows, rank_width, panel_width = row_basis.shape
    cluster_rows = coarse_sources.shape[0]
    cluster_count = cluster_rows * leaf_count
    far_share = far_blocks.shape[1]
    coarse_share = coarse_blocks.shape[1]
    near_share = near_blocks.shape[1]
    vector_share = vector_count // owner_count
    first_leaf = leaf_index * leaf_rows
    flat_width = vector_count * rank_width
    x_blocks = adjoint_in.reshape(vector_count, leaf_rows, panel_width)
    leaf_up = jnp.einsum(
        "klp,lrp->lkr", x_blocks, row_basis, preferred_element_type=jnp.float32
    ).astype(jnp.bfloat16)
    branch = jnp.einsum("lkr,lrc->lkc", leaf_up, row_transfer, preferred_element_type=jnp.float32)
    branch_flat = branch.reshape(leaf_rows, flat_width)
    cluster_ids = lax.broadcasted_iota(jnp.int32, (cluster_count, leaf_rows), 0)
    members = (cluster_ids == parents[None, :]).astype(jnp.float32)
    partial_up = jnp.dot(members, branch_flat, precision=lax.Precision.HIGHEST)
    cluster_up = lax.psum(partial_up, "leaf").astype(jnp.bfloat16)
    cluster_up = cluster_up.reshape(cluster_count, vector_count, rank_width)
    my_coarse = lax.dynamic_slice_in_dim(
        coarse_sources, owner_index * coarse_share, coarse_share, 1
    )
    coarse_rows = jnp.take(cluster_up, my_coarse.reshape(-1), axis=0)
    coarse_rows = coarse_rows.reshape(cluster_rows, coarse_share, vector_count, rank_width)
    cluster_part = jnp.einsum(
        "cjkr,cjrs->cks", coarse_rows, coarse_blocks, preferred_element_type=jnp.float32
    )
    cluster_part = cluster_part.reshape(cluster_rows, flat_width)
    my_far = lax.dynamic_slice_in_dim(far_sources, owner_index * far_share, far_share, 1)
    shard_rows = lax.all_gather(leaf_up, "leaf", axis=0, tiled=True)
    picked = jnp.take(shard_rows, my_far.reshape(-1), axis=0)
    picked = picked.reshape(leaf_rows, far_share, vector_count, rank_width)
    leaf_down_part = jnp.einsum(
        "ljkr,ljrs->lks", picked, far_blocks, preferred_element_type=jnp.float32
    )
    leaf_down_part = leaf_down_part.reshape(leaf_rows, flat_width)
    padded = with_halo(adjoint_in, (("leaf", 1),), REACH * panel_width)
    padded = padded.reshape(vector_count, leaf_rows + 2 * REACH, panel_width)
    my_near = lax.dynamic_slice_in_dim(near_sources, owner_index * near_share, near_share, 1)
    local_near = (my_near - first_leaf + REACH).reshape(-1)
    near_rows = jnp.take(padded, local_near, axis=1).reshape(
        vector_count, leaf_rows, near_share, panel_width
    )
    near_part = jnp.einsum(
        "kljp,ljpq->klq", near_rows, near_blocks, preferred_element_type=jnp.float32
    )
    near_part = near_part.reshape(vector_count, leaf_rows * panel_width)
    leaf_down, cluster_down, near_sum = (
        lax.psum_scatter(leaf_down_part, ("vec", "lvl"), scatter_dimension=1, tiled=True),
        lax.psum_scatter(cluster_part, ("vec", "lvl"), scatter_dimension=1, tiled=True),
        lax.psum_scatter(near_part, ("vec", "lvl"), scatter_dimension=0, tiled=True),
    )
    down_table = lax.all_gather(cluster_down.astype(jnp.bfloat16), "leaf", axis=0, tiled=True)
    pushed = jnp.take(down_table, parents, axis=0).reshape(leaf_rows, vector_share, rank_width)
    carried = jnp.einsum("lkc,lrc->lkr", pushed, col_transfer, preferred_element_type=jnp.float32)
    leaf_total = (leaf_down.reshape(leaf_rows, vector_share, rank_width) + carried).astype(
        jnp.bfloat16
    )
    far_out = jnp.einsum("lkr,lrp->klp", leaf_total, col_basis, preferred_element_type=jnp.float32)
    far_out = far_out.reshape(vector_share, leaf_rows * panel_width)
    return (far_out + near_sum).astype(jnp.bfloat16)


def up_kernel(x_ref, basis_ref, transfer_ref, coarse_ref, parents_ref,
              msg_ref, packed_ref, edge_ref, sums):
    leaves, rank, panel = basis_ref.shape
    z, c = lax.axis_index("leaf"), lax.axis_index("lvl")
    width = REACH * panel
    start = jnp.where((z + c) % 2 == 0, leaves * panel - width, 0)
    edge_ref[...] = x_ref[:, pl.ds(pl.multiple_of(start, 128), width)]
    share = coarse_ref.shape[1]
    for j in range(share):
        packed_ref[j] = jnp.concatenate([coarse_ref[0, j], coarse_ref[1, j]], axis=-1)
    sums[...] = jnp.zeros_like(sums)
    ups = []
    for l in range(leaves):
        up = dot_t(x_ref[:, l * panel:(l + 1) * panel], basis_ref[l]).astype(BF)
        ups.append(up)
        parent = parents_ref[l]
        sums[parent] = sums[parent] + dot(up, transfer_ref[l])
    for p in range(leaves // 2):
        msg_ref[p] = jnp.concatenate([ups[2 * p], ups[2 * p + 1]], axis=-1)
    for p in range(sums.shape[0] // 2):
        msg_ref[leaves // 2 + p] = jnp.concatenate(
            [sums[2 * p], sums[2 * p + 1]], axis=-1
        ).astype(BF)


def near_kernel(sources_ref, x_ref, mine_ref, other_ref, blocks_hbm, out_ref,
                table, blocks, sems):
    leaves, share, panel = blocks.shape[0], blocks.shape[1], blocks.shape[2]
    z, c = lax.axis_index("leaf"), lax.axis_index("lvl")
    owner = lax.axis_index("vec") * 2 + c
    copies = [
        pltpu.make_async_copy(blocks_hbm.at[l], blocks.at[l], sems.at[l]) for l in range(leaves)
    ]
    for copy in copies:
        copy.start()
    for l in range(leaves):
        table[REACH + l] = x_ref[:, l * panel:(l + 1) * panel]
    high = (z + c) % 2 == 0
    top, bottom = leaves + REACH, 0
    at_mine = jnp.where(high, top, bottom)
    at_other = jnp.where(high, bottom, top)
    for i in range(REACH):
        table[at_mine + i] = mine_ref[:, i * panel:(i + 1) * panel]
        table[at_other + i] = other_ref[:, i * panel:(i + 1) * panel]
    for l in range(leaves):
        rows = [
            table[sources_ref[l, owner * share + j] - z * leaves + REACH] for j in range(share)
        ]
        copies[l].wait()
        out_ref[l] = dot(jnp.concatenate(rows, axis=-1), blocks[l].reshape(share * panel, panel))


def coarse_kernel(sources_ref, own_ref, a_ref, la_ref, b_ref, lb_ref,
                  p_own, p_lvl, p_vec, p_diag, out_ref, table):
    pairs = own_ref.shape[0] // 2
    share = p_own.shape[0]
    c = lax.axis_index("lvl")
    me = lax.axis_index("vec") * 2 + c
    rank = own_ref.shape[1]
    for p in range(pairs):
        q = pairs + p
        across = jnp.where(c == 1, b_ref[q].astype(F32), lb_ref[q].astype(F32))
        total = (own_ref[q].astype(F32) + a_ref[q].astype(F32)) + (la_ref[q].astype(F32) + across)
        table[p] = total.astype(BF)
        table[pairs + p] = swap_halves(total).astype(BF)
    low = low_half((rank, 2 * rank))
    acc = jnp.zeros((2 * rank, 2 * rank), F32)
    for flip, blocks in ((0, p_own), (1, p_lvl), (2, p_vec), (3, p_diag)):
        base = (me ^ flip) * share
        rows = []
        for cluster in range(2):
            lanes = []
            for j in range(0, share, 2):
                s0 = sources_ref[cluster, base + j]
                s1 = sources_ref[cluster, base + j + 1]
                first = table[(s0 & 1) * pairs + (s0 >> 1)]
                second = table[(1 - (s1 & 1)) * pairs + (s1 >> 1)]
                lanes.append(jnp.where(low, first, second))
            rows.append(jnp.concatenate(lanes, axis=-1))
        acc = acc + dot(
            jnp.concatenate(rows, axis=0), blocks[...].reshape(share * rank, 2 * rank)
        )
    out_ref[...] = jnp.where(low, acc[:rank], acc[rank:]).astype(BF)


def down_kernel(sources_ref, parents_ref, own_ref, a_ref, la_ref, b_ref, lb_ref,
                blocks_ref, down_ref, got_ref, transfer_ref, basis_ref, near_ref,
                send_ref, keep_ref, table, total):
    leaves, share, rank, _ = blocks_ref.shape
    panel = basis_ref.shape[2]
    pairs = leaves // 2
    z, v, c = lax.axis_index("leaf"), lax.axis_index("vec"), lax.axis_index("lvl")
    owner = v * 2 + c
    far = jnp.where(c == 1, 3, 1)
    near = jnp.where(c == 1, 1, 3)
    count = 4 * pairs
    for p in range(pairs):
        x = own_ref[p].astype(F32)
        table[p] = own_ref[p]
        table[count + p] = swap_halves(x).astype(BF)
        x = a_ref[p].astype(F32)
        table[far * pairs + p] = a_ref[p]
        table[count + far * pairs + p] = swap_halves(x).astype(BF)
        x = la_ref[p].astype(F32)
        table[near * pairs + p] = la_ref[p]
        table[count + near * pairs + p] = swap_halves(x).astype(BF)
        x = jnp.where(c == 1, b_ref[p].astype(F32), lb_ref[p].astype(F32))
        table[2 * pairs + p] = x.astype(BF)
        table[count + 2 * pairs + p] = swap_halves(x).astype(BF)
    low = low_half((rank, 2 * rank))
    lane = lax.broadcasted_iota(jnp.int32, (rank, 2 * rank), 1)
    distance = jnp.where(c == 1, jnp.where(v == 1, 2, 3), jnp.where(v == 1, 1, 0))
    home = z ^ distance
    down = jnp.where(distance == 0, down_ref[...].astype(F32), got_ref[...].astype(F32))
    for l in range(leaves):
        lanes = []
        for j in range(0, share, 2):
            s0 = sources_ref[l, owner * share + j]
            s1 = sources_ref[l, owner * share + j + 1]
            at0 = ((s0 // leaves) ^ z) * pairs + ((s0 % leaves) >> 1)
            at1 = ((s1 // leaves) ^ z) * pairs + ((s1 % leaves) >> 1)
            first = table[(s0 & 1) * count + at0]
            second = table[(1 - (s1 & 1)) * count + at1]
            lanes.append(jnp.where(low, first, second))
        part = dot(jnp.concatenate(lanes, axis=-1), blocks_ref[l].reshape(share * rank, rank))
        parent = parents_ref[l]
        begin = jnp.where((parent >> 1) == home, (parent & 1) * rank, -2 * rank)
        pushed = jnp.where((lane >= begin) & (lane < begin + rank), down, 0.0).astype(BF)
        weight = transfer_ref[l]
        part = part + dot_t(pushed, jnp.concatenate([weight, weight], axis=-1))
        total[:, l * panel:(l + 1) * panel] = near_ref[l] + dot(part.astype(BF), basis_ref[l])
    rows = keep_ref.shape[1]
    for w in range(2):
        mine = pl.multiple_of((w * 2 + c) * rows, rows)
        theirs = pl.multiple_of((w * 2 + 1 - c) * rows, rows)
        keep_ref[w] = total[pl.ds(mine, rows), :]
        send_ref[w] = total[pl.ds(theirs, rows), :].astype(BF)


def merge_kernel(keep_ref, got_ref, send_ref, rest_ref):
    v = lax.axis_index("vec")
    send_ref[...] = (keep_ref[1 - v] + got_ref[1 - v].astype(F32)).astype(BF)
    rest_ref[...] = keep_ref[v] + got_ref[v].astype(F32)


def swap(x, route):
    axes = ("leaf", "vec", "lvl")
    zs, vs, cs = (lax.axis_size(a) for a in axes)
    pairs = []
    for z in range(zs):
        for v in range(vs):
            for c in range(cs):
                target = route(z, v, c)
                if target is not None:
                    tz, tv, tc = target
                    pairs.append(((z * vs + v) * cs + c, (tz * vs + tv) * cs + tc))
    return lax.ppermute(x, axes, pairs)


def on_device_paired(
    adjoint_in,
    row_basis,
    col_basis,
    row_transfer,
    col_transfer,
    parents,
    far_sources,
    far_blocks,
    coarse_sources,
    coarse_blocks,
    near_sources,
    near_blocks,
):
    vectors = adjoint_in.shape[0]
    leaves, rank, panel = row_basis.shape
    clusters = coarse_sources.shape[0] * 4
    coarse_share = coarse_blocks.shape[1]
    near_share = near_blocks.shape[1]
    width = leaves * panel
    params = pltpu.CompilerParams(vmem_limit_bytes=LIMIT)
    wide = 2 * rank
    messages = leaves // 2 + clusters // 2
    msg, packed, edge = pl.pallas_call(
        up_kernel,
        out_shape=(
            jax.ShapeDtypeStruct((messages, vectors, wide), BF),
            jax.ShapeDtypeStruct((coarse_share, rank, wide), BF),
            jax.ShapeDtypeStruct((vectors, REACH * panel), BF),
        ),
        in_specs=[VMEM] * 4 + [SMEM],
        out_specs=(VMEM,) * 3,
        scratch_shapes=[pltpu.VMEM((clusters, vectors, rank), F32)],
        compiler_params=params,
        name="up",
    )(adjoint_in, row_basis, row_transfer, coarse_blocks, parents)

    def other_core(z, v, c):
        return z, v, 1 - c

    def other_chip(z, v, c):
        return z, 1 - v, c

    a = swap(msg, lambda z, v, c: (z ^ (3 if c else 1), v, c))
    b = swap(msg, lambda z, v, c: (z ^ 2, v, c) if c else None)

    def neighbour(z, v, c):
        target = z + 1 if (z + c) % 2 == 0 else z - 1
        return (target, v, c) if 0 <= target < 4 else None

    halo = swap(edge, neighbour)
    halo_other = swap(halo, other_core)
    p_lvl = swap(packed, other_core)
    p_vec = swap(packed, other_chip)
    p_diag = swap(p_vec, other_core)
    near = pl.pallas_call(
        near_kernel,
        out_shape=jax.ShapeDtypeStruct((leaves, vectors, panel), F32),
        in_specs=[SMEM] + [VMEM] * 3 + [ANY],
        out_specs=VMEM,
        scratch_shapes=[
            pltpu.VMEM((leaves + 2 * REACH, vectors, panel), BF),
            pltpu.VMEM((leaves, near_share, panel, panel), BF),
            pltpu.SemaphoreType.DMA((leaves,)),
        ],
        compiler_params=params,
        name="near",
    )(near_sources, adjoint_in, halo, halo_other, near_blocks)
    la = swap(a, other_core)
    lb = swap(b, lambda z, v, c: (z, v, 0) if c else None)
    down = pl.pallas_call(
        coarse_kernel,
        out_shape=jax.ShapeDtypeStruct((vectors, wide), BF),
        in_specs=[SMEM] + [VMEM] * 9,
        out_specs=VMEM,
        scratch_shapes=[pltpu.VMEM((clusters, vectors, wide), BF)],
        compiler_params=params,
        name="coarse",
    )(coarse_sources, msg, a, la, b, lb, packed, p_lvl, p_vec, p_diag)

    def home(z, v, c):
        distance = (2 if v else 3) if c else (1 if v else 0)
        return (z ^ distance, v, c) if distance else None

    got = swap(down, home)
    rows = vectors // 4
    send, keep = pl.pallas_call(
        down_kernel,
        out_shape=(
            jax.ShapeDtypeStruct((2, rows, width), BF),
            jax.ShapeDtypeStruct((2, rows, width), F32),
        ),
        in_specs=[SMEM] * 2 + [VMEM] * 11,
        out_specs=(VMEM,) * 2,
        scratch_shapes=[
            pltpu.VMEM((4 * leaves, vectors, wide), BF),
            pltpu.VMEM((vectors, width), F32),
        ],
        compiler_params=params,
        name="down",
    )(far_sources, parents, msg, a, la, b, lb, far_blocks, down, got, col_transfer, col_basis, near)
    came = swap(send, other_core)
    send, rest = pl.pallas_call(
        merge_kernel,
        out_shape=(
            jax.ShapeDtypeStruct((rows, width), BF),
            jax.ShapeDtypeStruct((rows, width), F32),
        ),
        in_specs=[VMEM] * 2,
        out_specs=(VMEM,) * 2,
        compiler_params=params,
        name="merge",
    )(keep, came)
    came = swap(send, other_chip)
    return (rest + came.astype(F32)).astype(BF)


def solution(mesh):
    in_specs = (
        P("groups", "leaf"),
        P(("groups", "leaf"), None, None),
        P(("groups", "leaf"), None, None),
        P(("groups", "leaf"), None, None),
        P(("groups", "leaf"), None, None),
        P(("groups", "leaf")),
        P(("groups", "leaf"), None),
        P(("groups", "leaf"), ("vec", "lvl"), None, None),
        P(("groups", "leaf"), None),
        P(("groups", "leaf"), ("vec", "lvl"), None, None),
        P(("groups", "leaf"), None),
        P(("groups", "leaf"), ("vec", "lvl"), None, None),
    )
    out_specs = P(("groups", "vec", "lvl"), "leaf")
    sizes = tuple(mesh.shape[a] for a in ("leaf", "vec", "lvl"))
    body = on_device_paired if sizes == (4, 2, 2) else on_device_general
    return jax.shard_map(
        body, mesh=mesh, in_specs=in_specs, out_specs=out_specs, check_vma=False
    )
```

```python
import jax
import jax.numpy as jnp
from jax import lax
from jax.experimental import pallas as pl
from jax.experimental.pallas import tpu as pltpu
from jax.sharding import PartitionSpec as P

REACH = 2
BF = jnp.bfloat16
F32 = jnp.float32
VMEM = pl.BlockSpec(memory_space=pltpu.VMEM)
SMEM = pl.BlockSpec(memory_space=pltpu.SMEM)
HBM = pl.BlockSpec(memory_space=pltpu.HBM)
LIMIT = 32 << 20


def cost(us):
    return pl.CostEstimate(flops=int(us * 1e9), bytes_accessed=1024, transcendentals=0)


def dot(a, b):
    return jnp.dot(a, b, preferred_element_type=F32)


def dot_t(a, b):
    return lax.dot_general(a, b, (((1,), (1,)), ((), ())), preferred_element_type=F32)


def low_half(shape):
    return lax.broadcasted_iota(jnp.int32, shape, len(shape) - 1) < shape[-1] // 2


def swap_halves(x):
    half = x.shape[-1] // 2
    return jnp.concatenate([x[..., half:], x[..., :half]], axis=-1)


def with_halo(block, sides, width):
    for axis, dim in sides:
        count = lax.axis_size(axis)
        forward = [(i, i + 1) for i in range(count - 1)]
        backward = [(target, source) for source, target in forward]
        low = lax.ppermute(
            lax.slice_in_dim(block, block.shape[dim] - width, None, axis=dim), axis, forward
        )
        high = lax.ppermute(lax.slice_in_dim(block, 0, width, axis=dim), axis, backward)
        block = jnp.concatenate([low, block, high], axis=dim)
    return block


def on_device_general(
    adjoint_in,
    row_basis,
    col_basis,
    row_transfer,
    col_transfer,
    parents,
    far_sources,
    far_blocks,
    coarse_sources,
    coarse_blocks,
    near_sources,
    near_blocks,
):
    owner_count = lax.axis_size(("vec", "lvl"))
    owner_index = lax.axis_index(("vec", "lvl"))
    leaf_index = lax.axis_index("leaf")
    leaf_count = lax.axis_size("leaf")
    vector_count = adjoint_in.shape[0]
    leaf_rows, rank_width, panel_width = row_basis.shape
    cluster_rows = coarse_sources.shape[0]
    cluster_count = cluster_rows * leaf_count
    far_share = far_blocks.shape[1]
    coarse_share = coarse_blocks.shape[1]
    near_share = near_blocks.shape[1]
    vector_share = vector_count // owner_count
    first_leaf = leaf_index * leaf_rows
    flat_width = vector_count * rank_width
    x_blocks = adjoint_in.reshape(vector_count, leaf_rows, panel_width)
    leaf_up = jnp.einsum(
        "klp,lrp->lkr", x_blocks, row_basis, preferred_element_type=jnp.float32
    ).astype(jnp.bfloat16)
    branch = jnp.einsum("lkr,lrc->lkc", leaf_up, row_transfer, preferred_element_type=jnp.float32)
    branch_flat = branch.reshape(leaf_rows, flat_width)
    cluster_ids = lax.broadcasted_iota(jnp.int32, (cluster_count, leaf_rows), 0)
    members = (cluster_ids == parents[None, :]).astype(jnp.float32)
    partial_up = jnp.dot(members, branch_flat, precision=lax.Precision.HIGHEST)
    cluster_up = lax.psum(partial_up, "leaf").astype(jnp.bfloat16)
    cluster_up = cluster_up.reshape(cluster_count, vector_count, rank_width)
    my_coarse = lax.dynamic_slice_in_dim(
        coarse_sources, owner_index * coarse_share, coarse_share, 1
    )
    coarse_rows = jnp.take(cluster_up, my_coarse.reshape(-1), axis=0)
    coarse_rows = coarse_rows.reshape(cluster_rows, coarse_share, vector_count, rank_width)
    cluster_part = jnp.einsum(
        "cjkr,cjrs->cks", coarse_rows, coarse_blocks, preferred_element_type=jnp.float32
    )
    cluster_part = cluster_part.reshape(cluster_rows, flat_width)
    my_far = lax.dynamic_slice_in_dim(far_sources, owner_index * far_share, far_share, 1)
    shard_rows = lax.all_gather(leaf_up, "leaf", axis=0, tiled=True)
    picked = jnp.take(shard_rows, my_far.reshape(-1), axis=0)
    picked = picked.reshape(leaf_rows, far_share, vector_count, rank_width)
    leaf_down_part = jnp.einsum(
        "ljkr,ljrs->lks", picked, far_blocks, preferred_element_type=jnp.float32
    )
    leaf_down_part = leaf_down_part.reshape(leaf_rows, flat_width)
    padded = with_halo(adjoint_in, (("leaf", 1),), REACH * panel_width)
    padded = padded.reshape(vector_count, leaf_rows + 2 * REACH, panel_width)
    my_near = lax.dynamic_slice_in_dim(near_sources, owner_index * near_share, near_share, 1)
    local_near = (my_near - first_leaf + REACH).reshape(-1)
    near_rows = jnp.take(padded, local_near, axis=1).reshape(
        vector_count, leaf_rows, near_share, panel_width
    )
    near_part = jnp.einsum(
        "kljp,ljpq->klq", near_rows, near_blocks, preferred_element_type=jnp.float32
    )
    near_part = near_part.reshape(vector_count, leaf_rows * panel_width)
    leaf_down, cluster_down, near_sum = (
        lax.psum_scatter(leaf_down_part, ("vec", "lvl"), scatter_dimension=1, tiled=True),
        lax.psum_scatter(cluster_part, ("vec", "lvl"), scatter_dimension=1, tiled=True),
        lax.psum_scatter(near_part, ("vec", "lvl"), scatter_dimension=0, tiled=True),
    )
    down_table = lax.all_gather(cluster_down.astype(jnp.bfloat16), "leaf", axis=0, tiled=True)
    pushed = jnp.take(down_table, parents, axis=0).reshape(leaf_rows, vector_share, rank_width)
    carried = jnp.einsum("lkc,lrc->lkr", pushed, col_transfer, preferred_element_type=jnp.float32)
    leaf_total = (leaf_down.reshape(leaf_rows, vector_share, rank_width) + carried).astype(
        jnp.bfloat16
    )
    far_out = jnp.einsum("lkr,lrp->klp", leaf_total, col_basis, preferred_element_type=jnp.float32)
    far_out = far_out.reshape(vector_share, leaf_rows * panel_width)
    return (far_out + near_sum).astype(jnp.bfloat16)


def up_kernel(x_hbm, basis_hbm, transfer_hbm, parents_hbm, msg_ref, short_ref,
              x_ref, basis_ref, transfer_ref, parents_ref, sums, sems):
    copies = [
        pltpu.make_async_copy(a, b, sems.at[i])
        for i, (a, b) in enumerate((
            (x_hbm, x_ref),
            (basis_hbm, basis_ref),
            (parents_hbm, parents_ref),
            (transfer_hbm, transfer_ref),
        ))
    ]
    for copy in copies:
        copy.start()
    sums[...] = jnp.zeros_like(sums)
    leaves, rank, panel = basis_ref.shape
    z, c = lax.axis_index("leaf"), lax.axis_index("lvl")
    pairs = leaves // 2
    clusters = sums.shape[0]
    copies[0].wait()
    start = jnp.where((z + c) % 2 == 0, (leaves - REACH) * panel, 0)
    base = pairs + clusters // 2
    for i in range(REACH * panel // (2 * rank)):
        at = pl.multiple_of(start + i * 2 * rank, 2 * rank)
        msg_ref[base + i] = x_ref[:, pl.ds(at, 2 * rank)]
    copies[1].wait()
    ups = [
        dot_t(x_ref[:, l * panel:(l + 1) * panel], basis_ref[l]).astype(BF)
        for l in range(leaves)
    ]
    for p in range(pairs):
        msg_ref[p] = short_ref[p] = jnp.concatenate([ups[2 * p], ups[2 * p + 1]], axis=-1)
    copies[2].wait()
    copies[3].wait()
    for l in range(leaves):
        parent = parents_ref[l]
        sums[parent] = sums[parent] + dot(ups[l], transfer_ref[l])
    for p in range(clusters // 2):
        merged = jnp.concatenate([sums[2 * p], sums[2 * p + 1]], axis=-1).astype(BF)
        msg_ref[pairs + p] = short_ref[pairs + p] = merged


def near_kernel(sources_hbm, x_ref, a_ref, la_ref, blocks_ref, out_ref, sources_ref, table, sem):
    copy = pltpu.make_async_copy(sources_hbm, sources_ref, sem)
    copy.start()
    leaves, share, panel, _ = blocks_ref.shape
    z, c = lax.axis_index("leaf"), lax.axis_index("lvl")
    owner = lax.axis_index("vec") * 2 + c
    high = (z + c) % 2 == 0
    top, bottom = leaves + REACH, 0
    at_a = jnp.where(high, top, bottom)
    at_la = jnp.where(high, bottom, top)
    lanes = a_ref.shape[2]
    parts = panel // lanes
    base = a_ref.shape[0] - REACH * parts
    for i in range(REACH):
        for w in range(parts):
            table[at_a + i, :, w * lanes:(w + 1) * lanes] = a_ref[base + i * parts + w]
            table[at_la + i, :, w * lanes:(w + 1) * lanes] = la_ref[base + i * parts + w]
    for l in range(leaves):
        table[REACH + l] = x_ref[:, l * panel:(l + 1) * panel]
    copy.wait()
    for l in range(leaves):
        rows = [
            table[sources_ref[l, owner * share + j] - z * leaves + REACH] for j in range(share)
        ]
        out_ref[l] = dot(
            jnp.concatenate(rows, axis=-1), blocks_ref[l].reshape(share * panel, panel)
        )


def coarse_kernel(sources_hbm, own_ref, a_ref, la_ref, b_ref, lb_ref,
                  p_own, p_lvl, p_vec, p_diag, out_ref, sources_ref, table, sem):
    copy = pltpu.make_async_copy(sources_hbm, sources_ref, sem)
    copy.start()
    _, share, rank, _ = p_own.shape
    pairs = table.shape[0] // 2
    c = lax.axis_index("lvl")
    me = lax.axis_index("vec") * 2 + c
    for p in range(pairs):
        q = pairs + p
        across = jnp.where(c == 1, b_ref[q].astype(F32), lb_ref[q].astype(F32))
        total = (own_ref[q].astype(F32) + a_ref[q].astype(F32)) + (la_ref[q].astype(F32) + across)
        table[p] = total.astype(BF)
        table[pairs + p] = swap_halves(total).astype(BF)
    low = low_half((out_ref.shape[0], 2 * rank))
    accs = [jnp.zeros((out_ref.shape[0], rank), F32) for _ in range(2)]
    copy.wait()
    for flip, blocks in enumerate((p_own, p_lvl, p_vec, p_diag)):
        base = (me ^ flip) * share
        for cluster in range(2):
            lanes = []
            for j in range(0, share, 2):
                s0 = sources_ref[cluster, base + j]
                s1 = sources_ref[cluster, base + j + 1]
                first = table[(s0 & 1) * pairs + (s0 >> 1)]
                second = table[(1 - (s1 & 1)) * pairs + (s1 >> 1)]
                lanes.append(jnp.where(low, first, second))
            accs[cluster] = accs[cluster] + dot(
                jnp.concatenate(lanes, axis=-1), blocks[cluster].reshape(share * rank, rank)
            )
    out_ref[...] = jnp.concatenate(accs, axis=-1).astype(BF)


def down_kernel(sources_hbm, parents_hbm, own_ref, a_ref, la_ref, b_ref, lb_ref,
                blocks_ref, down_ref, got_ref, transfer_ref, basis_ref, near_ref,
                send_ref, keep_ref, sources_ref, parents_ref, table, total, sems):
    copies = [
        pltpu.make_async_copy(a, b, sems.at[i])
        for i, (a, b) in enumerate((
            (sources_hbm, sources_ref),
            (parents_hbm, parents_ref),
        ))
    ]
    for copy in copies:
        copy.start()
    leaves, share, rank, _ = blocks_ref.shape
    panel = basis_ref.shape[2]
    pairs = leaves // 2
    z, v, c = lax.axis_index("leaf"), lax.axis_index("vec"), lax.axis_index("lvl")
    owner = v * 2 + c
    far = jnp.where(c == 1, 3, 1)
    near = jnp.where(c == 1, 1, 3)
    count = 4 * pairs
    for p in range(pairs):
        x = own_ref[p].astype(F32)
        table[p] = own_ref[p]
        table[count + p] = swap_halves(x).astype(BF)
        x = a_ref[p].astype(F32)
        table[far * pairs + p] = a_ref[p]
        table[count + far * pairs + p] = swap_halves(x).astype(BF)
        x = la_ref[p].astype(F32)
        table[near * pairs + p] = la_ref[p]
        table[count + near * pairs + p] = swap_halves(x).astype(BF)
        x = jnp.where(c == 1, b_ref[p].astype(F32), lb_ref[p].astype(F32))
        table[2 * pairs + p] = x.astype(BF)
        table[count + 2 * pairs + p] = swap_halves(x).astype(BF)
    low = low_half((own_ref.shape[1], 2 * rank))
    lane = lax.broadcasted_iota(jnp.int32, low.shape, 1)
    distance = jnp.where(c == 1, jnp.where(v == 1, 2, 3), jnp.where(v == 1, 1, 0))
    home = z ^ distance
    down = jnp.where(distance == 0, down_ref[...].astype(F32), got_ref[...].astype(F32))
    for copy in copies:
        copy.wait()
    for l in range(leaves):
        lanes = []
        for j in range(0, share, 2):
            s0 = sources_ref[l, owner * share + j]
            s1 = sources_ref[l, owner * share + j + 1]
            at0 = ((s0 // leaves) ^ z) * pairs + ((s0 % leaves) >> 1)
            at1 = ((s1 // leaves) ^ z) * pairs + ((s1 % leaves) >> 1)
            first = table[(s0 & 1) * count + at0]
            second = table[(1 - (s1 & 1)) * count + at1]
            lanes.append(jnp.where(low, first, second))
        part = dot(jnp.concatenate(lanes, axis=-1), blocks_ref[l].reshape(share * rank, rank))
        parent = parents_ref[l]
        begin = jnp.where((parent >> 1) == home, (parent & 1) * rank, -2 * rank)
        pushed = jnp.where((lane >= begin) & (lane < begin + rank), down, 0.0).astype(BF)
        weight = transfer_ref[l]
        part = part + dot_t(pushed, jnp.concatenate([weight, weight], axis=-1))
        total[:, l * panel:(l + 1) * panel] = near_ref[l] + dot(part.astype(BF), basis_ref[l])
    rows = keep_ref.shape[1]
    for w in range(2):
        mine = pl.multiple_of((w * 2 + c) * rows, rows)
        theirs = pl.multiple_of((w * 2 + 1 - c) * rows, rows)
        keep_ref[w] = total[pl.ds(mine, rows), :]
        send_ref[w] = total[pl.ds(theirs, rows), :].astype(BF)


def merge_kernel(keep_ref, got_ref, send_ref, rest_ref):
    v = lax.axis_index("vec")
    send_ref[...] = (keep_ref[1 - v] + got_ref[1 - v].astype(F32)).astype(BF)
    rest_ref[...] = keep_ref[v] + got_ref[v].astype(F32)


def in_hbm(*arrays):
    return [pltpu.with_memory_space_constraint(x, pltpu.HBM) for x in arrays]


def swap(x, route):
    axes = ("leaf", "vec", "lvl")
    zs, vs, cs = (lax.axis_size(a) for a in axes)
    pairs = []
    for z in range(zs):
        for v in range(vs):
            for c in range(cs):
                target = route(z, v, c)
                if target is not None:
                    tz, tv, tc = target
                    pairs.append(((z * vs + v) * cs + c, (tz * vs + tv) * cs + tc))
    return lax.ppermute(x, axes, pairs)


def on_device_paired(
    adjoint_in,
    row_basis,
    col_basis,
    row_transfer,
    col_transfer,
    parents,
    far_sources,
    far_blocks,
    coarse_sources,
    coarse_blocks,
    near_sources,
    near_blocks,
):
    vectors = adjoint_in.shape[0]
    leaves, rank, panel = row_basis.shape
    clusters = coarse_sources.shape[0] * 4
    coarse_share = coarse_blocks.shape[1]
    width = leaves * panel
    params = pltpu.CompilerParams(vmem_limit_bytes=LIMIT)
    wide = 2 * rank
    messages = leaves // 2 + clusters // 2 + REACH * panel // wide

    def other_core(z, v, c):
        return z, v, 1 - c

    def other_chip(z, v, c):
        return z, 1 - v, c

    p_lvl = swap(coarse_blocks, other_core)
    p_vec = swap(coarse_blocks, other_chip)
    msg, short = pl.pallas_call(
        up_kernel,
        out_shape=(
            jax.ShapeDtypeStruct((messages, vectors, wide), BF),
            jax.ShapeDtypeStruct((leaves // 2 + clusters // 2, vectors, wide), BF),
        ),
        in_specs=[HBM] * 4,
        out_specs=(VMEM,) * 2,
        scratch_shapes=[
            pltpu.VMEM(adjoint_in.shape, BF),
            pltpu.VMEM(row_basis.shape, BF),
            pltpu.VMEM(row_transfer.shape, BF),
            pltpu.SMEM(parents.shape, jnp.int32),
            pltpu.VMEM((clusters, vectors, rank), F32),
            pltpu.SemaphoreType.DMA((4,)),
        ],
        compiler_params=params,
        cost_estimate=cost(1.5),
        name="up",
    )(*in_hbm(adjoint_in, row_basis, row_transfer, parents))
    a = swap(msg, lambda z, v, c: (z ^ (3 if c else 1), v, c))
    b = swap(short, lambda z, v, c: (z ^ 2, v, c) if c else None)
    p_diag = swap(p_vec, other_core)
    la = swap(a, other_core)
    near = pl.pallas_call(
        near_kernel,
        out_shape=jax.ShapeDtypeStruct((leaves, vectors, panel), F32),
        in_specs=[HBM] + [VMEM] * 4,
        out_specs=VMEM,
        scratch_shapes=[
            pltpu.SMEM(near_sources.shape, jnp.int32),
            pltpu.VMEM((leaves + 2 * REACH, vectors, panel), BF),
            pltpu.SemaphoreType.DMA(()),
        ],
        compiler_params=params,
        cost_estimate=cost(2.5),
        name="near",
    )(*in_hbm(near_sources), adjoint_in, a, la, near_blocks)
    b, near = lax.optimization_barrier((b, near))
    lb = swap(b, lambda z, v, c: (z, v, 0) if c else None)
    down = pl.pallas_call(
        coarse_kernel,
        out_shape=jax.ShapeDtypeStruct((vectors, wide), BF),
        in_specs=[HBM] + [VMEM] * 9,
        out_specs=VMEM,
        scratch_shapes=[
            pltpu.SMEM(coarse_sources.shape, jnp.int32),
            pltpu.VMEM((clusters, vectors, wide), BF),
            pltpu.SemaphoreType.DMA(()),
        ],
        compiler_params=params,
        cost_estimate=cost(1.0),
        name="coarse",
    )(*in_hbm(coarse_sources), msg, a, la, b, lb, coarse_blocks, p_lvl, p_vec, p_diag)

    def home(z, v, c):
        distance = (2 if v else 3) if c else (1 if v else 0)
        return (z ^ distance, v, c) if distance else None

    got = swap(down, home)
    rows = vectors // 4
    send, keep = pl.pallas_call(
        down_kernel,
        out_shape=(
            jax.ShapeDtypeStruct((2, rows, width), BF),
            jax.ShapeDtypeStruct((2, rows, width), F32),
        ),
        in_specs=[HBM] * 2 + [VMEM] * 11,
        out_specs=(VMEM,) * 2,
        scratch_shapes=[
            pltpu.SMEM(far_sources.shape, jnp.int32),
            pltpu.SMEM(parents.shape, jnp.int32),
            pltpu.VMEM((4 * leaves, vectors, wide), BF),
            pltpu.VMEM((vectors, width), F32),
            pltpu.SemaphoreType.DMA((2,)),
        ],
        compiler_params=params,
        cost_estimate=cost(2.5),
        name="down",
    )(*in_hbm(far_sources, parents), msg, a, la, b, lb, far_blocks, down, got, col_transfer, col_basis, near)
    came = swap(send, other_core)
    send, rest = pl.pallas_call(
        merge_kernel,
        out_shape=(
            jax.ShapeDtypeStruct((rows, width), BF),
            jax.ShapeDtypeStruct((rows, width), F32),
        ),
        in_specs=[VMEM] * 2,
        out_specs=(VMEM,) * 2,
        compiler_params=params,
        cost_estimate=cost(0.6),
        name="merge",
    )(keep, came)
    came = swap(send, other_chip)
    return (rest + came.astype(F32)).astype(BF)


def solution(mesh):
    in_specs = (
        P("groups", "leaf"),
        P(("groups", "leaf"), None, None),
        P(("groups", "leaf"), None, None),
        P(("groups", "leaf"), None, None),
        P(("groups", "leaf"), None, None),
        P(("groups", "leaf")),
        P(("groups", "leaf"), None),
        P(("groups", "leaf"), ("vec", "lvl"), None, None),
        P(("groups", "leaf"), None),
        P(("groups", "leaf"), ("vec", "lvl"), None, None),
        P(("groups", "leaf"), None),
        P(("groups", "leaf"), ("vec", "lvl"), None, None),
    )
    out_specs = P(("groups", "vec", "lvl"), "leaf")
    sizes = tuple(mesh.shape[a] for a in ("leaf", "vec", "lvl"))
    body = on_device_paired if sizes == (4, 2, 2) else on_device_general
    return jax.shard_map(
        body, mesh=mesh, in_specs=in_specs, out_specs=out_specs, check_vma=False
    )
```

```python
import jax
import jax.numpy as jnp
from jax import lax
from jax.experimental import pallas as pl
from jax.experimental.pallas import tpu as pltpu
from jax.sharding import PartitionSpec as P

REACH = 2
BF = jnp.bfloat16
F32 = jnp.float32
VMEM = pl.BlockSpec(memory_space=pltpu.VMEM)
SMEM = pl.BlockSpec(memory_space=pltpu.SMEM)
HBM = pl.BlockSpec(memory_space=pltpu.HBM)
LIMIT = 32 << 20


def cost(us):
    return pl.CostEstimate(flops=int(us * 1e9), bytes_accessed=1024, transcendentals=0)


def dot(a, b):
    return jnp.dot(a, b, preferred_element_type=F32)


def dot_t(a, b):
    return lax.dot_general(a, b, (((1,), (1,)), ((), ())), preferred_element_type=F32)


def low_half(shape):
    return lax.broadcasted_iota(jnp.int32, shape, len(shape) - 1) < shape[-1] // 2


def swap_halves(x):
    half = x.shape[-1] // 2
    return jnp.concatenate([x[..., half:], x[..., :half]], axis=-1)


def with_halo(block, sides, width):
    for axis, dim in sides:
        count = lax.axis_size(axis)
        forward = [(i, i + 1) for i in range(count - 1)]
        backward = [(target, source) for source, target in forward]
        low = lax.ppermute(
            lax.slice_in_dim(block, block.shape[dim] - width, None, axis=dim), axis, forward
        )
        high = lax.ppermute(lax.slice_in_dim(block, 0, width, axis=dim), axis, backward)
        block = jnp.concatenate([low, block, high], axis=dim)
    return block


def on_device_general(
    adjoint_in,
    row_basis,
    col_basis,
    row_transfer,
    col_transfer,
    parents,
    far_sources,
    far_blocks,
    coarse_sources,
    coarse_blocks,
    near_sources,
    near_blocks,
):
    owner_count = lax.axis_size(("vec", "lvl"))
    owner_index = lax.axis_index(("vec", "lvl"))
    leaf_index = lax.axis_index("leaf")
    leaf_count = lax.axis_size("leaf")
    vector_count = adjoint_in.shape[0]
    leaf_rows, rank_width, panel_width = row_basis.shape
    cluster_rows = coarse_sources.shape[0]
    cluster_count = cluster_rows * leaf_count
    far_share = far_blocks.shape[1]
    coarse_share = coarse_blocks.shape[1]
    near_share = near_blocks.shape[1]
    vector_share = vector_count // owner_count
    first_leaf = leaf_index * leaf_rows
    flat_width = vector_count * rank_width
    x_blocks = adjoint_in.reshape(vector_count, leaf_rows, panel_width)
    leaf_up = jnp.einsum(
        "klp,lrp->lkr", x_blocks, row_basis, preferred_element_type=jnp.float32
    ).astype(jnp.bfloat16)
    branch = jnp.einsum("lkr,lrc->lkc", leaf_up, row_transfer, preferred_element_type=jnp.float32)
    branch_flat = branch.reshape(leaf_rows, flat_width)
    cluster_ids = lax.broadcasted_iota(jnp.int32, (cluster_count, leaf_rows), 0)
    members = (cluster_ids == parents[None, :]).astype(jnp.float32)
    partial_up = jnp.dot(members, branch_flat, precision=lax.Precision.HIGHEST)
    cluster_up = lax.psum(partial_up, "leaf").astype(jnp.bfloat16)
    cluster_up = cluster_up.reshape(cluster_count, vector_count, rank_width)
    my_coarse = lax.dynamic_slice_in_dim(
        coarse_sources, owner_index * coarse_share, coarse_share, 1
    )
    coarse_rows = jnp.take(cluster_up, my_coarse.reshape(-1), axis=0)
    coarse_rows = coarse_rows.reshape(cluster_rows, coarse_share, vector_count, rank_width)
    cluster_part = jnp.einsum(
        "cjkr,cjrs->cks", coarse_rows, coarse_blocks, preferred_element_type=jnp.float32
    )
    cluster_part = cluster_part.reshape(cluster_rows, flat_width)
    my_far = lax.dynamic_slice_in_dim(far_sources, owner_index * far_share, far_share, 1)
    shard_rows = lax.all_gather(leaf_up, "leaf", axis=0, tiled=True)
    picked = jnp.take(shard_rows, my_far.reshape(-1), axis=0)
    picked = picked.reshape(leaf_rows, far_share, vector_count, rank_width)
    leaf_down_part = jnp.einsum(
        "ljkr,ljrs->lks", picked, far_blocks, preferred_element_type=jnp.float32
    )
    leaf_down_part = leaf_down_part.reshape(leaf_rows, flat_width)
    padded = with_halo(adjoint_in, (("leaf", 1),), REACH * panel_width)
    padded = padded.reshape(vector_count, leaf_rows + 2 * REACH, panel_width)
    my_near = lax.dynamic_slice_in_dim(near_sources, owner_index * near_share, near_share, 1)
    local_near = (my_near - first_leaf + REACH).reshape(-1)
    near_rows = jnp.take(padded, local_near, axis=1).reshape(
        vector_count, leaf_rows, near_share, panel_width
    )
    near_part = jnp.einsum(
        "kljp,ljpq->klq", near_rows, near_blocks, preferred_element_type=jnp.float32
    )
    near_part = near_part.reshape(vector_count, leaf_rows * panel_width)
    leaf_down, cluster_down, near_sum = (
        lax.psum_scatter(leaf_down_part, ("vec", "lvl"), scatter_dimension=1, tiled=True),
        lax.psum_scatter(cluster_part, ("vec", "lvl"), scatter_dimension=1, tiled=True),
        lax.psum_scatter(near_part, ("vec", "lvl"), scatter_dimension=0, tiled=True),
    )
    down_table = lax.all_gather(cluster_down.astype(jnp.bfloat16), "leaf", axis=0, tiled=True)
    pushed = jnp.take(down_table, parents, axis=0).reshape(leaf_rows, vector_share, rank_width)
    carried = jnp.einsum("lkc,lrc->lkr", pushed, col_transfer, preferred_element_type=jnp.float32)
    leaf_total = (leaf_down.reshape(leaf_rows, vector_share, rank_width) + carried).astype(
        jnp.bfloat16
    )
    far_out = jnp.einsum("lkr,lrp->klp", leaf_total, col_basis, preferred_element_type=jnp.float32)
    far_out = far_out.reshape(vector_share, leaf_rows * panel_width)
    return (far_out + near_sum).astype(jnp.bfloat16)


def up_kernel(x_hbm, basis_hbm, transfer_hbm, coarse_hbm, parents_hbm,
              msg_ref, short_ref, packed_ref,
              x_ref, basis_ref, transfer_ref, coarse_ref, parents_ref, sums, sems):
    copies = [
        pltpu.make_async_copy(a, b, sems.at[i])
        for i, (a, b) in enumerate((
            (x_hbm, x_ref),
            (basis_hbm, basis_ref),
            (parents_hbm, parents_ref),
            (transfer_hbm, transfer_ref),
            (coarse_hbm, coarse_ref),
        ))
    ]
    for copy in copies:
        copy.start()
    sums[...] = jnp.zeros_like(sums)
    leaves, rank, panel = basis_ref.shape
    z, c = lax.axis_index("leaf"), lax.axis_index("lvl")
    pairs = leaves // 2
    clusters = sums.shape[0]
    copies[0].wait()
    start = jnp.where((z + c) % 2 == 0, (leaves - REACH) * panel, 0)
    base = pairs + clusters // 2
    for i in range(REACH * panel // (2 * rank)):
        at = pl.multiple_of(start + i * 2 * rank, 2 * rank)
        msg_ref[base + i] = x_ref[:, pl.ds(at, 2 * rank)]
    copies[1].wait()
    ups = [
        dot_t(x_ref[:, l * panel:(l + 1) * panel], basis_ref[l]).astype(BF)
        for l in range(leaves)
    ]
    for p in range(pairs):
        msg_ref[p] = short_ref[p] = jnp.concatenate([ups[2 * p], ups[2 * p + 1]], axis=-1)
    copies[2].wait()
    copies[3].wait()
    for l in range(leaves):
        parent = parents_ref[l]
        sums[parent] = sums[parent] + dot(ups[l], transfer_ref[l])
    for p in range(clusters // 2):
        merged = jnp.concatenate([sums[2 * p], sums[2 * p + 1]], axis=-1).astype(BF)
        msg_ref[pairs + p] = short_ref[pairs + p] = merged
    copies[4].wait()
    for j in range(coarse_ref.shape[1]):
        packed_ref[j] = jnp.concatenate([coarse_ref[0, j], coarse_ref[1, j]], axis=-1)


def coarse_kernel(sources_hbm, own_ref, a_ref, la_ref, b_ref, lb_ref,
                  p_own, p_lvl, p_vec, p_diag, out_ref, sources_ref, table, sem):
    copy = pltpu.make_async_copy(sources_hbm, sources_ref, sem)
    copy.start()
    share, rank, wide = p_own.shape
    vectors = out_ref.shape[0]
    pairs = table.shape[0] // 2
    c = lax.axis_index("lvl")
    me = lax.axis_index("vec") * 2 + c
    for p in range(pairs):
        q = pairs + p
        across = jnp.where(c == 1, b_ref[q].astype(F32), lb_ref[q].astype(F32))
        total = (own_ref[q].astype(F32) + a_ref[q].astype(F32)) + (la_ref[q].astype(F32) + across)
        table[p] = total.astype(BF)
        table[pairs + p] = swap_halves(total).astype(BF)
    low = low_half((vectors, wide))
    acc = jnp.zeros((2 * vectors, wide), F32)
    copy.wait()
    for flip, blocks in enumerate((p_own, p_lvl, p_vec, p_diag)):
        base = (me ^ flip) * share
        rows = []
        for cluster in range(2):
            lanes = []
            for j in range(0, share, 2):
                s0 = sources_ref[cluster, base + j]
                s1 = sources_ref[cluster, base + j + 1]
                first = table[(s0 & 1) * pairs + (s0 >> 1)]
                second = table[(1 - (s1 & 1)) * pairs + (s1 >> 1)]
                lanes.append(jnp.where(low, first, second))
            rows.append(jnp.concatenate(lanes, axis=-1))
        acc = acc + dot(jnp.concatenate(rows, axis=0), blocks[...].reshape(share * rank, wide))
    out_ref[...] = jnp.where(low, acc[:vectors], acc[vectors:]).astype(BF)


def local_kernel(near_hbm, far_hbm, own_ref, a_ref, la_ref, b_ref, lb_ref, x_ref,
                 near_blocks_ref, far_blocks_ref, near_ref, far_ref,
                 near_sources, far_sources, panels, table, sems):
    copies = [
        pltpu.make_async_copy(near_hbm, near_sources, sems.at[0]),
        pltpu.make_async_copy(far_hbm, far_sources, sems.at[1]),
    ]
    for copy in copies:
        copy.start()
    leaves, near_share, panel, _ = near_blocks_ref.shape
    far_share, rank = far_blocks_ref.shape[1:3]
    z, c = lax.axis_index("leaf"), lax.axis_index("lvl")
    owner = lax.axis_index("vec") * 2 + c
    high = (z + c) % 2 == 0
    top, bottom = leaves + REACH, 0
    at_a = jnp.where(high, top, bottom)
    at_la = jnp.where(high, bottom, top)
    lanes = a_ref.shape[2]
    parts = panel // lanes
    base = a_ref.shape[0] - REACH * parts
    for i in range(REACH):
        for w in range(parts):
            panels[at_a + i, :, w * lanes:(w + 1) * lanes] = a_ref[base + i * parts + w]
            panels[at_la + i, :, w * lanes:(w + 1) * lanes] = la_ref[base + i * parts + w]
    for l in range(leaves):
        panels[REACH + l] = x_ref[:, l * panel:(l + 1) * panel]
    pairs = leaves // 2
    far = jnp.where(c == 1, 3, 1)
    near = jnp.where(c == 1, 1, 3)
    count = 4 * pairs
    for p in range(pairs):
        x = own_ref[p].astype(F32)
        table[p] = own_ref[p]
        table[count + p] = swap_halves(x).astype(BF)
        x = a_ref[p].astype(F32)
        table[far * pairs + p] = a_ref[p]
        table[count + far * pairs + p] = swap_halves(x).astype(BF)
        x = la_ref[p].astype(F32)
        table[near * pairs + p] = la_ref[p]
        table[count + near * pairs + p] = swap_halves(x).astype(BF)
        x = jnp.where(c == 1, b_ref[p].astype(F32), lb_ref[p].astype(F32))
        table[2 * pairs + p] = x.astype(BF)
        table[count + 2 * pairs + p] = swap_halves(x).astype(BF)
    low = low_half((own_ref.shape[1], 2 * rank))
    for copy in copies:
        copy.wait()
    for l in range(leaves):
        rows = [
            panels[near_sources[l, owner * near_share + j] - z * leaves + REACH]
            for j in range(near_share)
        ]
        near_ref[l] = dot(
            jnp.concatenate(rows, axis=-1), near_blocks_ref[l].reshape(near_share * panel, panel)
        )
        rows = []
        for j in range(0, far_share, 2):
            s0 = far_sources[l, owner * far_share + j]
            s1 = far_sources[l, owner * far_share + j + 1]
            at0 = ((s0 // leaves) ^ z) * pairs + ((s0 % leaves) >> 1)
            at1 = ((s1 // leaves) ^ z) * pairs + ((s1 % leaves) >> 1)
            first = table[(s0 & 1) * count + at0]
            second = table[(1 - (s1 & 1)) * count + at1]
            rows.append(jnp.where(low, first, second))
        far_ref[l] = dot(
            jnp.concatenate(rows, axis=-1), far_blocks_ref[l].reshape(far_share * rank, rank)
        )


def down_kernel(parents_hbm, near_ref, far_ref, down_ref, got_ref, transfer_ref, basis_ref,
                send_ref, keep_ref, parents_ref, total, sem):
    copy = pltpu.make_async_copy(parents_hbm, parents_ref, sem)
    copy.start()
    leaves, rank, panel = basis_ref.shape
    z, v, c = lax.axis_index("leaf"), lax.axis_index("vec"), lax.axis_index("lvl")
    lane = lax.broadcasted_iota(jnp.int32, down_ref.shape, 1)
    distance = jnp.where(c == 1, jnp.where(v == 1, 2, 3), jnp.where(v == 1, 1, 0))
    home = z ^ distance
    down = jnp.where(distance == 0, down_ref[...].astype(F32), got_ref[...].astype(F32))
    copy.wait()
    for l in range(leaves):
        parent = parents_ref[l]
        begin = jnp.where((parent >> 1) == home, (parent & 1) * rank, -2 * rank)
        pushed = jnp.where((lane >= begin) & (lane < begin + rank), down, 0.0).astype(BF)
        weight = transfer_ref[l]
        part = far_ref[l] + dot_t(pushed, jnp.concatenate([weight, weight], axis=-1))
        total[:, l * panel:(l + 1) * panel] = near_ref[l] + dot(part.astype(BF), basis_ref[l])
    rows = keep_ref.shape[1]
    for w in range(2):
        mine = pl.multiple_of((w * 2 + c) * rows, rows)
        theirs = pl.multiple_of((w * 2 + 1 - c) * rows, rows)
        keep_ref[w] = total[pl.ds(mine, rows), :]
        send_ref[w] = total[pl.ds(theirs, rows), :].astype(BF)


def merge_kernel(keep_ref, got_ref, send_ref, rest_ref):
    v = lax.axis_index("vec")
    send_ref[...] = (keep_ref[1 - v] + got_ref[1 - v].astype(F32)).astype(BF)
    rest_ref[...] = keep_ref[v] + got_ref[v].astype(F32)


def in_hbm(*arrays):
    return [pltpu.with_memory_space_constraint(x, pltpu.HBM) for x in arrays]


def swap(x, route):
    axes = ("leaf", "vec", "lvl")
    zs, vs, cs = (lax.axis_size(a) for a in axes)
    pairs = []
    for z in range(zs):
        for v in range(vs):
            for c in range(cs):
                target = route(z, v, c)
                if target is not None:
                    tz, tv, tc = target
                    pairs.append(((z * vs + v) * cs + c, (tz * vs + tv) * cs + tc))
    return lax.ppermute(x, axes, pairs)


def on_device_paired(
    adjoint_in,
    row_basis,
    col_basis,
    row_transfer,
    col_transfer,
    parents,
    far_sources,
    far_blocks,
    coarse_sources,
    coarse_blocks,
    near_sources,
    near_blocks,
):
    vectors = adjoint_in.shape[0]
    leaves, rank, panel = row_basis.shape
    clusters = coarse_sources.shape[0] * 4
    coarse_share = coarse_blocks.shape[1]
    width = leaves * panel
    params = pltpu.CompilerParams(vmem_limit_bytes=LIMIT)
    wide = 2 * rank
    messages = leaves // 2 + clusters // 2 + REACH * panel // wide

    def other_core(z, v, c):
        return z, v, 1 - c

    def other_chip(z, v, c):
        return z, 1 - v, c

    msg, short, packed = pl.pallas_call(
        up_kernel,
        out_shape=(
            jax.ShapeDtypeStruct((messages, vectors, wide), BF),
            jax.ShapeDtypeStruct((leaves // 2 + clusters // 2, vectors, wide), BF),
            jax.ShapeDtypeStruct((coarse_blocks.shape[1], rank, wide), BF),
        ),
        in_specs=[HBM] * 5,
        out_specs=(VMEM,) * 3,
        scratch_shapes=[
            pltpu.VMEM(adjoint_in.shape, BF),
            pltpu.VMEM(row_basis.shape, BF),
            pltpu.VMEM(row_transfer.shape, BF),
            pltpu.VMEM(coarse_blocks.shape, BF),
            pltpu.SMEM(parents.shape, jnp.int32),
            pltpu.VMEM((clusters, vectors, rank), F32),
            pltpu.SemaphoreType.DMA((5,)),
        ],
        compiler_params=params,
        cost_estimate=cost(1.5),
        name="up",
    )(*in_hbm(adjoint_in, row_basis, row_transfer, coarse_blocks, parents))
    a = swap(msg, lambda z, v, c: (z ^ (3 if c else 1), v, c))
    b = swap(short, lambda z, v, c: (z ^ 2, v, c) if c else None)
    p_lvl = swap(packed, other_core)
    p_vec = swap(packed, other_chip)
    p_diag = swap(p_vec, other_core)
    a, b = lax.optimization_barrier((a, b))
    la = swap(a, other_core)
    lb = swap(b, lambda z, v, c: (z, v, 0) if c else None)
    down = pl.pallas_call(
        coarse_kernel,
        out_shape=jax.ShapeDtypeStruct((vectors, wide), BF),
        in_specs=[HBM] + [VMEM] * 9,
        out_specs=VMEM,
        scratch_shapes=[
            pltpu.SMEM(coarse_sources.shape, jnp.int32),
            pltpu.VMEM((clusters, vectors, wide), BF),
            pltpu.SemaphoreType.DMA(()),
        ],
        compiler_params=params,
        cost_estimate=cost(1.0),
        name="coarse",
    )(*in_hbm(coarse_sources), msg, a, la, b, lb, packed, p_lvl, p_vec, p_diag)

    def home(z, v, c):
        distance = (2 if v else 3) if c else (1 if v else 0)
        return (z ^ distance, v, c) if distance else None

    got = swap(down, home)
    near, far = pl.pallas_call(
        local_kernel,
        out_shape=(
            jax.ShapeDtypeStruct((leaves, vectors, panel), F32),
            jax.ShapeDtypeStruct((leaves, vectors, rank), F32),
        ),
        in_specs=[HBM] * 2 + [VMEM] * 8,
        out_specs=(VMEM,) * 2,
        scratch_shapes=[
            pltpu.SMEM(near_sources.shape, jnp.int32),
            pltpu.SMEM(far_sources.shape, jnp.int32),
            pltpu.VMEM((leaves + 2 * REACH, vectors, panel), BF),
            pltpu.VMEM((4 * leaves, vectors, wide), BF),
            pltpu.SemaphoreType.DMA((2,)),
        ],
        compiler_params=params,
        cost_estimate=cost(4.0),
        name="local",
    )(*in_hbm(near_sources, far_sources), msg, a, la, b, lb, adjoint_in, near_blocks, far_blocks)
    rows = vectors // 4
    send, keep = pl.pallas_call(
        down_kernel,
        out_shape=(
            jax.ShapeDtypeStruct((2, rows, width), BF),
            jax.ShapeDtypeStruct((2, rows, width), F32),
        ),
        in_specs=[HBM] + [VMEM] * 6,
        out_specs=(VMEM,) * 2,
        scratch_shapes=[
            pltpu.SMEM(parents.shape, jnp.int32),
            pltpu.VMEM((vectors, width), F32),
            pltpu.SemaphoreType.DMA(()),
        ],
        compiler_params=params,
        cost_estimate=cost(1.0),
        name="down",
    )(*in_hbm(parents), near, far, down, got, col_transfer, col_basis)
    came = swap(send, other_core)
    send, rest = pl.pallas_call(
        merge_kernel,
        out_shape=(
            jax.ShapeDtypeStruct((rows, width), BF),
            jax.ShapeDtypeStruct((rows, width), F32),
        ),
        in_specs=[VMEM] * 2,
        out_specs=(VMEM,) * 2,
        compiler_params=params,
        cost_estimate=cost(0.6),
        name="merge",
    )(keep, came)
    came = swap(send, other_chip)
    return (rest + came.astype(F32)).astype(BF)


def solution(mesh):
    in_specs = (
        P("groups", "leaf"),
        P(("groups", "leaf"), None, None),
        P(("groups", "leaf"), None, None),
        P(("groups", "leaf"), None, None),
        P(("groups", "leaf"), None, None),
        P(("groups", "leaf")),
        P(("groups", "leaf"), None),
        P(("groups", "leaf"), ("vec", "lvl"), None, None),
        P(("groups", "leaf"), None),
        P(("groups", "leaf"), ("vec", "lvl"), None, None),
        P(("groups", "leaf"), None),
        P(("groups", "leaf"), ("vec", "lvl"), None, None),
    )
    out_specs = P(("groups", "vec", "lvl"), "leaf")
    sizes = tuple(mesh.shape[a] for a in ("leaf", "vec", "lvl"))
    body = on_device_paired if sizes == (4, 2, 2) else on_device_general
    return jax.shard_map(
        body, mesh=mesh, in_specs=in_specs, out_specs=out_specs, check_vma=False
    )
```

```python
import jax
import jax.numpy as jnp
from jax import lax
from jax.experimental import pallas as pl
from jax.experimental.pallas import tpu as pltpu
from jax.sharding import PartitionSpec as P

REACH = 2
BF = jnp.bfloat16
F32 = jnp.float32
VMEM = pl.BlockSpec(memory_space=pltpu.VMEM)
SMEM = pl.BlockSpec(memory_space=pltpu.SMEM)
HBM = pl.BlockSpec(memory_space=pltpu.HBM)
LIMIT = 32 << 20


def cost(us):
    return pl.CostEstimate(flops=int(us * 1e9), bytes_accessed=1024, transcendentals=0)


def dot(a, b):
    return jnp.dot(a, b, preferred_element_type=F32)


def dot_t(a, b):
    return lax.dot_general(a, b, (((1,), (1,)), ((), ())), preferred_element_type=F32)


def low_half(shape):
    return lax.broadcasted_iota(jnp.int32, shape, len(shape) - 1) < shape[-1] // 2


def swap_halves(x):
    half = x.shape[-1] // 2
    return jnp.concatenate([x[..., half:], x[..., :half]], axis=-1)


def with_halo(block, sides, width):
    for axis, dim in sides:
        count = lax.axis_size(axis)
        forward = [(i, i + 1) for i in range(count - 1)]
        backward = [(target, source) for source, target in forward]
        low = lax.ppermute(
            lax.slice_in_dim(block, block.shape[dim] - width, None, axis=dim), axis, forward
        )
        high = lax.ppermute(lax.slice_in_dim(block, 0, width, axis=dim), axis, backward)
        block = jnp.concatenate([low, block, high], axis=dim)
    return block


def on_device_general(
    adjoint_in,
    row_basis,
    col_basis,
    row_transfer,
    col_transfer,
    parents,
    far_sources,
    far_blocks,
    coarse_sources,
    coarse_blocks,
    near_sources,
    near_blocks,
):
    owner_count = lax.axis_size(("vec", "lvl"))
    owner_index = lax.axis_index(("vec", "lvl"))
    leaf_index = lax.axis_index("leaf")
    leaf_count = lax.axis_size("leaf")
    vector_count = adjoint_in.shape[0]
    leaf_rows, rank_width, panel_width = row_basis.shape
    cluster_rows = coarse_sources.shape[0]
    cluster_count = cluster_rows * leaf_count
    far_share = far_blocks.shape[1]
    coarse_share = coarse_blocks.shape[1]
    near_share = near_blocks.shape[1]
    vector_share = vector_count // owner_count
    first_leaf = leaf_index * leaf_rows
    flat_width = vector_count * rank_width
    x_blocks = adjoint_in.reshape(vector_count, leaf_rows, panel_width)
    leaf_up = jnp.einsum(
        "klp,lrp->lkr", x_blocks, row_basis, preferred_element_type=jnp.float32
    ).astype(jnp.bfloat16)
    branch = jnp.einsum("lkr,lrc->lkc", leaf_up, row_transfer, preferred_element_type=jnp.float32)
    branch_flat = branch.reshape(leaf_rows, flat_width)
    cluster_ids = lax.broadcasted_iota(jnp.int32, (cluster_count, leaf_rows), 0)
    members = (cluster_ids == parents[None, :]).astype(jnp.float32)
    partial_up = jnp.dot(members, branch_flat, precision=lax.Precision.HIGHEST)
    cluster_up = lax.psum(partial_up, "leaf").astype(jnp.bfloat16)
    cluster_up = cluster_up.reshape(cluster_count, vector_count, rank_width)
    my_coarse = lax.dynamic_slice_in_dim(
        coarse_sources, owner_index * coarse_share, coarse_share, 1
    )
    coarse_rows = jnp.take(cluster_up, my_coarse.reshape(-1), axis=0)
    coarse_rows = coarse_rows.reshape(cluster_rows, coarse_share, vector_count, rank_width)
    cluster_part = jnp.einsum(
        "cjkr,cjrs->cks", coarse_rows, coarse_blocks, preferred_element_type=jnp.float32
    )
    cluster_part = cluster_part.reshape(cluster_rows, flat_width)
    my_far = lax.dynamic_slice_in_dim(far_sources, owner_index * far_share, far_share, 1)
    shard_rows = lax.all_gather(leaf_up, "leaf", axis=0, tiled=True)
    picked = jnp.take(shard_rows, my_far.reshape(-1), axis=0)
    picked = picked.reshape(leaf_rows, far_share, vector_count, rank_width)
    leaf_down_part = jnp.einsum(
        "ljkr,ljrs->lks", picked, far_blocks, preferred_element_type=jnp.float32
    )
    leaf_down_part = leaf_down_part.reshape(leaf_rows, flat_width)
    padded = with_halo(adjoint_in, (("leaf", 1),), REACH * panel_width)
    padded = padded.reshape(vector_count, leaf_rows + 2 * REACH, panel_width)
    my_near = lax.dynamic_slice_in_dim(near_sources, owner_index * near_share, near_share, 1)
    local_near = (my_near - first_leaf + REACH).reshape(-1)
    near_rows = jnp.take(padded, local_near, axis=1).reshape(
        vector_count, leaf_rows, near_share, panel_width
    )
    near_part = jnp.einsum(
        "kljp,ljpq->klq", near_rows, near_blocks, preferred_element_type=jnp.float32
    )
    near_part = near_part.reshape(vector_count, leaf_rows * panel_width)
    leaf_down, cluster_down, near_sum = (
        lax.psum_scatter(leaf_down_part, ("vec", "lvl"), scatter_dimension=1, tiled=True),
        lax.psum_scatter(cluster_part, ("vec", "lvl"), scatter_dimension=1, tiled=True),
        lax.psum_scatter(near_part, ("vec", "lvl"), scatter_dimension=0, tiled=True),
    )
    down_table = lax.all_gather(cluster_down.astype(jnp.bfloat16), "leaf", axis=0, tiled=True)
    pushed = jnp.take(down_table, parents, axis=0).reshape(leaf_rows, vector_share, rank_width)
    carried = jnp.einsum("lkc,lrc->lkr", pushed, col_transfer, preferred_element_type=jnp.float32)
    leaf_total = (leaf_down.reshape(leaf_rows, vector_share, rank_width) + carried).astype(
        jnp.bfloat16
    )
    far_out = jnp.einsum("lkr,lrp->klp", leaf_total, col_basis, preferred_element_type=jnp.float32)
    far_out = far_out.reshape(vector_share, leaf_rows * panel_width)
    return (far_out + near_sum).astype(jnp.bfloat16)


def up_kernel(x_hbm, basis_hbm, transfer_hbm, parents_hbm, coarse_hbm,
              msg_ref, short_ref, packed_ref,
              x_ref, basis_ref, transfer_ref, parents_ref, coarse_ref, sums, sems):
    copies = [
        pltpu.make_async_copy(a, b, sems.at[i])
        for i, (a, b) in enumerate((
            (x_hbm, x_ref),
            (basis_hbm, basis_ref),
            (parents_hbm, parents_ref),
            (transfer_hbm, transfer_ref),
            (coarse_hbm, coarse_ref),
        ))
    ]
    for copy in copies:
        copy.start()
    sums[...] = jnp.zeros_like(sums)
    leaves, rank, panel = basis_ref.shape
    z, c = lax.axis_index("leaf"), lax.axis_index("lvl")
    pairs = leaves // 2
    clusters = sums.shape[0]
    copies[0].wait()
    start = jnp.where((z + c) % 2 == 0, (leaves - REACH) * panel, 0)
    base = pairs + clusters // 2
    for i in range(REACH * panel // (2 * rank)):
        at = pl.multiple_of(start + i * 2 * rank, 2 * rank)
        msg_ref[base + i] = x_ref[:, pl.ds(at, 2 * rank)]
    copies[1].wait()
    ups = [
        dot_t(x_ref[:, l * panel:(l + 1) * panel], basis_ref[l]).astype(BF)
        for l in range(leaves)
    ]
    for p in range(pairs):
        msg_ref[p] = short_ref[p] = jnp.concatenate([ups[2 * p], ups[2 * p + 1]], axis=-1)
    copies[2].wait()
    copies[3].wait()
    branches = [dot(ups[l], transfer_ref[l]) for l in range(leaves)]
    for l in range(leaves):
        parent = parents_ref[l]
        sums[parent] = sums[parent] + branches[l]
    for p in range(clusters // 2):
        merged = jnp.concatenate([sums[2 * p], sums[2 * p + 1]], axis=-1).astype(BF)
        msg_ref[pairs + p] = short_ref[pairs + p] = merged
    copies[4].wait()
    for j in range(coarse_ref.shape[1]):
        packed_ref[j] = jnp.concatenate([coarse_ref[0, j], coarse_ref[1, j]], axis=-1)


def gate_kernel(after_ref, out_ref):
    out_ref[...] = jnp.zeros_like(out_ref)


def join_kernel(a_ref, b_ref, gate_ref, out_ref):
    count = a_ref.shape[0]
    out_ref[:count] = a_ref[...]
    out_ref[count:] = b_ref[...]


def coarse_kernel(sources_hbm, own_ref, a_ref, b_ref, other_ref, p_own, p_lvl, out_ref,
                  sources_ref, table, sem):
    copy = pltpu.make_async_copy(sources_hbm, sources_ref, sem)
    copy.start()
    share, rank, wide = p_own.shape
    vectors = out_ref.shape[0]
    pairs = table.shape[0] // 2
    count = a_ref.shape[0]
    me = lax.axis_index("vec") * 2 + lax.axis_index("lvl")
    for p in range(pairs):
        q = b_ref.shape[0] - pairs + p
        rest = b_ref[q].astype(F32) + other_ref[count + q].astype(F32)
        total = (own_ref[q].astype(F32) + a_ref[q].astype(F32)) + (
            other_ref[q].astype(F32) + rest
        )
        table[p] = total.astype(BF)
        table[pairs + p] = swap_halves(total).astype(BF)
    low = low_half((vectors, wide))
    acc = jnp.zeros((2 * vectors, wide), F32)
    copy.wait()
    for flip, blocks in enumerate((p_own, p_lvl)):
        base = (me ^ flip) * share
        rows = []
        for cluster in range(2):
            lanes = []
            for j in range(0, share, 2):
                s0 = sources_ref[cluster, base + j]
                s1 = sources_ref[cluster, base + j + 1]
                first = table[(s0 & 1) * pairs + (s0 >> 1)]
                second = table[(1 - (s1 & 1)) * pairs + (s1 >> 1)]
                lanes.append(jnp.where(low, first, second))
            rows.append(jnp.concatenate(lanes, axis=-1))
        acc = acc + dot(jnp.concatenate(rows, axis=0), blocks[...].reshape(share * rank, wide))
    out_ref[...] = jnp.where(low, acc[:vectors], acc[vectors:]).astype(BF)


def near_rows(sources, owner, z, l, leaves, share):
    return [sources[l, owner * share + j] - z * leaves + REACH for j in range(share)]


def prep_kernel(near_hbm, x_ref, near_blocks_ref, transfer_ref, basis_ref,
                near_ref, weight_ref, near_sources, panels, sem):
    copy = pltpu.make_async_copy(near_hbm, near_sources, sem)
    copy.start()
    leaves, share, panel, _ = near_blocks_ref.shape
    z = lax.axis_index("leaf")
    owner = lax.axis_index("vec") * 2 + lax.axis_index("lvl")
    for l in range(leaves):
        panels[REACH + l] = x_ref[:, l * panel:(l + 1) * panel]
    for l in range(leaves):
        weight = lax.dot_general(
            transfer_ref[l], basis_ref[l], (((0,), (0,)), ((), ())), preferred_element_type=F32
        ).astype(BF)
        weight_ref[l] = jnp.concatenate([weight, weight], axis=0)
    copy.wait()
    for l in range(REACH, leaves - REACH):
        rows = [panels[i] for i in near_rows(near_sources, owner, z, l, leaves, share)]
        near_ref[l - REACH] = dot(
            jnp.concatenate(rows, axis=-1), near_blocks_ref[l].reshape(share * panel, panel)
        )


def local_kernel(near_hbm, far_hbm, own_ref, a_ref, b_ref, other_ref, x_ref,
                 near_blocks_ref, far_blocks_ref, basis_ref, near_ref, total_ref,
                 near_sources, far_sources, panels, table, sems):
    copies = [
        pltpu.make_async_copy(near_hbm, near_sources, sems.at[0]),
        pltpu.make_async_copy(far_hbm, far_sources, sems.at[1]),
    ]
    for copy in copies:
        copy.start()
    leaves, near_share, panel, _ = near_blocks_ref.shape
    far_share, rank = far_blocks_ref.shape[1:3]
    z, c = lax.axis_index("leaf"), lax.axis_index("lvl")
    owner = lax.axis_index("vec") * 2 + c
    high = (z + c) % 2 == 0
    top, bottom = leaves + REACH, 0
    at_mine = jnp.where(high, top, bottom)
    at_other = jnp.where(high, bottom, top)
    lanes = a_ref.shape[2]
    base = b_ref.shape[0]
    parts = panel // lanes
    count = a_ref.shape[0]
    for i in range(REACH):
        for w in range(parts):
            where = slice(w * lanes, (w + 1) * lanes)
            panels[at_mine + i, :, where] = a_ref[base + i * parts + w]
            panels[at_other + i, :, where] = other_ref[base + i * parts + w]
    for l in range(leaves):
        panels[REACH + l] = x_ref[:, l * panel:(l + 1) * panel]
    pairs = leaves // 2
    at_a = jnp.where(c == 1, 3, 1) * pairs
    at_o = jnp.where(c == 1, 1, 3) * pairs
    half = 4 * pairs
    for p in range(pairs):
        third = b_ref[p].astype(F32) + other_ref[count + p].astype(F32)
        for at, x in (
            (p, own_ref[p].astype(F32)),
            (2 * pairs + p, third),
            (at_a + p, a_ref[p].astype(F32)),
            (at_o + p, other_ref[p].astype(F32)),
        ):
            table[at] = x.astype(BF)
            table[half + at] = swap_halves(x).astype(BF)
    mask = z * leaves
    low = low_half((own_ref.shape[1], 2 * rank))
    for copy in copies:
        copy.wait()
    parts = []
    for l in range(leaves):
        rows = []
        for j in range(0, far_share, 2):
            s0 = far_sources[l, owner * far_share + j]
            s1 = far_sources[l, owner * far_share + j + 1]
            first = table[((s0 ^ mask) >> 1) + (s0 & 1) * half]
            second = table[((s1 ^ mask) >> 1) + half - (s1 & 1) * half]
            rows.append(jnp.where(low, first, second))
        parts.append(
            dot(jnp.concatenate(rows, axis=-1), far_blocks_ref[l].reshape(far_share * rank, rank))
        )
    for l in range(leaves):
        if REACH <= l < leaves - REACH:
            close = near_ref[l - REACH]
        else:
            rows = [
                panels[i] for i in near_rows(near_sources, owner, z, l, leaves, near_share)
            ]
            close = dot(
                jnp.concatenate(rows, axis=-1),
                near_blocks_ref[l].reshape(near_share * panel, panel),
            )
        total_ref[l] = close + dot(parts[l].astype(BF), basis_ref[l])


def down_kernel(parents_hbm, total_ref, down_ref, first_ref, second_ref, weight_ref,
                send_ref, keep_ref, parents_ref, halves, sem):
    copy = pltpu.make_async_copy(parents_hbm, parents_ref, sem)
    copy.start()
    leaves, vectors, panel = total_ref.shape
    z, c = lax.axis_index("leaf"), lax.axis_index("lvl")
    low = low_half(down_ref.shape)
    zero = jnp.zeros(down_ref.shape, F32)
    own = down_ref[...].astype(F32)
    first = first_ref[...].astype(F32)
    second = second_ref[...].astype(F32)
    parts = [(0, jnp.where(c == 0, own, zero)), (1, second),
             (2, jnp.where(c == 0, first, zero)), (3, jnp.where(c == 0, zero, first))]
    for distance, x in parts:
        halves[2 * distance] = jnp.where(low, x, 0.0).astype(BF)
        halves[2 * distance + 1] = jnp.where(low, 0.0, x).astype(BF)
    rows = vectors // 4
    copy.wait()
    for l in range(leaves):
        parent = parents_ref[l]
        part = total_ref[l] + dot(halves[parent ^ (2 * z)], weight_ref[l])
        lanes = slice(l * panel, (l + 1) * panel)
        for w in range(2):
            even = part[2 * w * rows:(2 * w + 1) * rows]
            odd = part[(2 * w + 1) * rows:(2 * w + 2) * rows]
            keep_ref[w, :, lanes] = jnp.where(c == 0, even, odd)
            send_ref[w, :, lanes] = jnp.where(c == 0, odd, even).astype(BF)


def merge_kernel(keep_ref, got_ref, send_ref, rest_ref):
    v = lax.axis_index("vec")
    send_ref[...] = (keep_ref[1 - v] + got_ref[1 - v].astype(F32)).astype(BF)
    rest_ref[...] = keep_ref[v] + got_ref[v].astype(F32)


def in_hbm(*arrays):
    return [pltpu.with_memory_space_constraint(x, pltpu.HBM) for x in arrays]


def swap(x, route):
    axes = ("leaf", "vec", "lvl")
    zs, vs, cs = (lax.axis_size(a) for a in axes)
    pairs = []
    for z in range(zs):
        for v in range(vs):
            for c in range(cs):
                target = route(z, v, c)
                if target is not None:
                    tz, tv, tc = target
                    pairs.append(((z * vs + v) * cs + c, (tz * vs + tv) * cs + tc))
    return lax.ppermute(x, axes, pairs)


def on_device_paired(
    adjoint_in,
    row_basis,
    col_basis,
    row_transfer,
    col_transfer,
    parents,
    far_sources,
    far_blocks,
    coarse_sources,
    coarse_blocks,
    near_sources,
    near_blocks,
):
    vectors = adjoint_in.shape[0]
    leaves, rank, panel = row_basis.shape
    clusters = coarse_sources.shape[0] * 4
    width = leaves * panel
    params = pltpu.CompilerParams(vmem_limit_bytes=LIMIT)
    wide = 2 * rank
    messages = leaves // 2 + clusters // 2
    edges = REACH * panel // wide

    def other_core(z, v, c):
        return z, v, 1 - c

    def other_chip(z, v, c):
        return z, 1 - v, c

    msg, short, packed = pl.pallas_call(
        up_kernel,
        out_shape=(
            jax.ShapeDtypeStruct((messages + edges, vectors, wide), BF),
            jax.ShapeDtypeStruct((messages, vectors, wide), BF),
            jax.ShapeDtypeStruct((coarse_blocks.shape[1], rank, wide), BF),
        ),
        in_specs=[HBM] * 5,
        out_specs=(VMEM,) * 3,
        scratch_shapes=[
            pltpu.VMEM(adjoint_in.shape, BF),
            pltpu.VMEM(row_basis.shape, BF),
            pltpu.VMEM(row_transfer.shape, BF),
            pltpu.SMEM(parents.shape, jnp.int32),
            pltpu.VMEM(coarse_blocks.shape, BF),
            pltpu.VMEM((clusters, vectors, rank), F32),
            pltpu.SemaphoreType.DMA((5,)),
        ],
        compiler_params=params,
        cost_estimate=cost(1.5),
        name="up",
    )(*in_hbm(adjoint_in, row_basis, row_transfer, parents, coarse_blocks))
    a = swap(msg, lambda z, v, c: (z ^ (3 if c else 1), v, c))
    b = swap(short, lambda z, v, c: (z ^ 2, v, c) if c else None)
    p_lvl = swap(packed, other_core)
    near, weight = pl.pallas_call(
        prep_kernel,
        out_shape=(
            jax.ShapeDtypeStruct((leaves - 2 * REACH, vectors, panel), F32),
            jax.ShapeDtypeStruct((leaves, wide, panel), BF),
        ),
        in_specs=[HBM] + [VMEM] * 4,
        out_specs=(VMEM,) * 2,
        scratch_shapes=[
            pltpu.SMEM(near_sources.shape, jnp.int32),
            pltpu.VMEM((leaves + 2 * REACH, vectors, panel), BF),
            pltpu.SemaphoreType.DMA(()),
        ],
        compiler_params=params,
        cost_estimate=cost(1.5),
        name="prep",
    )(*in_hbm(near_sources), adjoint_in, near_blocks, col_transfer, col_basis)
    gate = pl.pallas_call(
        gate_kernel,
        out_shape=jax.ShapeDtypeStruct((8, 128), F32),
        in_specs=[pl.BlockSpec(memory_space=pl.ANY)],
        out_specs=VMEM,
        compiler_params=params,
        cost_estimate=cost(0.1),
        name="gate",
    )(p_lvl)
    joined = pl.pallas_call(
        join_kernel,
        out_shape=jax.ShapeDtypeStruct((2 * messages + edges, vectors, wide), BF),
        in_specs=[VMEM] * 3,
        out_specs=VMEM,
        compiler_params=params,
        cost_estimate=cost(0.5),
        name="join",
    )(a, b, gate)
    joined, near, weight = lax.optimization_barrier((joined, near, weight))
    other = swap(joined, other_core)
    down = pl.pallas_call(
        coarse_kernel,
        out_shape=jax.ShapeDtypeStruct((vectors, wide), BF),
        in_specs=[HBM] + [VMEM] * 6,
        out_specs=VMEM,
        scratch_shapes=[
            pltpu.SMEM(coarse_sources.shape, jnp.int32),
            pltpu.VMEM((clusters, vectors, wide), BF),
            pltpu.SemaphoreType.DMA(()),
        ],
        compiler_params=params,
        cost_estimate=cost(1.0),
        name="coarse",
    )(coarse_sources, msg, a, b, other, packed, p_lvl)
    first = swap(down, lambda z, v, c: (z ^ (3 if c else 2), v, c))
    second = swap(down, lambda z, v, c: (z ^ 1, v, c) if c else None)
    total = pl.pallas_call(
        local_kernel,
        out_shape=jax.ShapeDtypeStruct((leaves, vectors, panel), F32),
        in_specs=[HBM] * 2 + [VMEM] * 9,
        out_specs=VMEM,
        scratch_shapes=[
            pltpu.SMEM(near_sources.shape, jnp.int32),
            pltpu.SMEM(far_sources.shape, jnp.int32),
            pltpu.VMEM((leaves + 2 * REACH, vectors, panel), BF),
            pltpu.VMEM((4 * leaves, vectors, wide), BF),
            pltpu.SemaphoreType.DMA((2,)),
        ],
        compiler_params=params,
        cost_estimate=cost(4.0),
        name="local",
    )(
        near_sources, far_sources,
        msg, a, b, other, adjoint_in, near_blocks, far_blocks, col_basis, near,
    )
    rows = vectors // 4
    send, keep = pl.pallas_call(
        down_kernel,
        out_shape=(
            jax.ShapeDtypeStruct((2, rows, width), BF),
            jax.ShapeDtypeStruct((2, rows, width), F32),
        ),
        in_specs=[HBM] + [VMEM] * 5,
        out_specs=(VMEM,) * 2,
        scratch_shapes=[
            pltpu.SMEM(parents.shape, jnp.int32),
            pltpu.VMEM((8, vectors, wide), BF),
            pltpu.SemaphoreType.DMA(()),
        ],
        compiler_params=params,
        cost_estimate=cost(1.0),
        name="down",
    )(parents, total, down, first, second, weight)
    came = swap(send, other_core)
    send, rest = pl.pallas_call(
        merge_kernel,
        out_shape=(
            jax.ShapeDtypeStruct((rows, width), BF),
            jax.ShapeDtypeStruct((rows, width), F32),
        ),
        in_specs=[VMEM] * 2,
        out_specs=(VMEM,) * 2,
        compiler_params=params,
        cost_estimate=cost(0.6),
        name="merge",
    )(keep, came)
    came = swap(send, other_chip)
    return (rest + came.astype(F32)).astype(BF)


def solution(mesh):
    in_specs = (
        P("groups", "leaf"),
        P(("groups", "leaf"), None, None),
        P(("groups", "leaf"), None, None),
        P(("groups", "leaf"), None, None),
        P(("groups", "leaf"), None, None),
        P(("groups", "leaf")),
        P(("groups", "leaf"), None),
        P(("groups", "leaf"), ("vec", "lvl"), None, None),
        P(("groups", "leaf"), None),
        P(("groups", "leaf"), ("vec", "lvl"), None, None),
        P(("groups", "leaf"), None),
        P(("groups", "leaf"), ("vec", "lvl"), None, None),
    )
    out_specs = P(("groups", "vec", "lvl"), "leaf")
    sizes = tuple(mesh.shape[a] for a in ("leaf", "vec", "lvl"))
    body = on_device_paired if sizes == (4, 2, 2) else on_device_general
    return jax.shard_map(
        body, mesh=mesh, in_specs=in_specs, out_specs=out_specs, check_vma=False
    )
```

```python
import jax
import jax.numpy as jnp
from jax import lax
from jax.experimental import pallas as pl
from jax.experimental.pallas import tpu as pltpu
from jax.sharding import PartitionSpec as P

REACH = 2
BF = jnp.bfloat16
F32 = jnp.float32
VMEM = pl.BlockSpec(memory_space=pltpu.VMEM)
SMEM = pl.BlockSpec(memory_space=pltpu.SMEM)
HBM = pl.BlockSpec(memory_space=pltpu.HBM)
LIMIT = 32 << 20


def cost(us):
    return pl.CostEstimate(flops=int(us * 1e9), bytes_accessed=1024, transcendentals=0)


def dot(a, b):
    return jnp.dot(a, b, preferred_element_type=F32)


def dot_t(a, b):
    return lax.dot_general(a, b, (((1,), (1,)), ((), ())), preferred_element_type=F32)


def low_half(shape):
    return lax.broadcasted_iota(jnp.int32, shape, len(shape) - 1) < shape[-1] // 2


def swap_halves(x):
    half = x.shape[-1] // 2
    return jnp.concatenate([x[..., half:], x[..., :half]], axis=-1)


def with_halo(block, sides, width):
    for axis, dim in sides:
        count = lax.axis_size(axis)
        forward = [(i, i + 1) for i in range(count - 1)]
        backward = [(target, source) for source, target in forward]
        low = lax.ppermute(
            lax.slice_in_dim(block, block.shape[dim] - width, None, axis=dim), axis, forward
        )
        high = lax.ppermute(lax.slice_in_dim(block, 0, width, axis=dim), axis, backward)
        block = jnp.concatenate([low, block, high], axis=dim)
    return block


def on_device_general(
    adjoint_in,
    row_basis,
    col_basis,
    row_transfer,
    col_transfer,
    parents,
    far_sources,
    far_blocks,
    coarse_sources,
    coarse_blocks,
    near_sources,
    near_blocks,
):
    owner_count = lax.axis_size(("vec", "lvl"))
    owner_index = lax.axis_index(("vec", "lvl"))
    leaf_index = lax.axis_index("leaf")
    leaf_count = lax.axis_size("leaf")
    vector_count = adjoint_in.shape[0]
    leaf_rows, rank_width, panel_width = row_basis.shape
    cluster_rows = coarse_sources.shape[0]
    cluster_count = cluster_rows * leaf_count
    far_share = far_blocks.shape[1]
    coarse_share = coarse_blocks.shape[1]
    near_share = near_blocks.shape[1]
    vector_share = vector_count // owner_count
    first_leaf = leaf_index * leaf_rows
    flat_width = vector_count * rank_width
    x_blocks = adjoint_in.reshape(vector_count, leaf_rows, panel_width)
    leaf_up = jnp.einsum(
        "klp,lrp->lkr", x_blocks, row_basis, preferred_element_type=jnp.float32
    ).astype(jnp.bfloat16)
    branch = jnp.einsum("lkr,lrc->lkc", leaf_up, row_transfer, preferred_element_type=jnp.float32)
    branch_flat = branch.reshape(leaf_rows, flat_width)
    cluster_ids = lax.broadcasted_iota(jnp.int32, (cluster_count, leaf_rows), 0)
    members = (cluster_ids == parents[None, :]).astype(jnp.float32)
    partial_up = jnp.dot(members, branch_flat, precision=lax.Precision.HIGHEST)
    cluster_up = lax.psum(partial_up, "leaf").astype(jnp.bfloat16)
    cluster_up = cluster_up.reshape(cluster_count, vector_count, rank_width)
    my_coarse = lax.dynamic_slice_in_dim(
        coarse_sources, owner_index * coarse_share, coarse_share, 1
    )
    coarse_rows = jnp.take(cluster_up, my_coarse.reshape(-1), axis=0)
    coarse_rows = coarse_rows.reshape(cluster_rows, coarse_share, vector_count, rank_width)
    cluster_part = jnp.einsum(
        "cjkr,cjrs->cks", coarse_rows, coarse_blocks, preferred_element_type=jnp.float32
    )
    cluster_part = cluster_part.reshape(cluster_rows, flat_width)
    my_far = lax.dynamic_slice_in_dim(far_sources, owner_index * far_share, far_share, 1)
    shard_rows = lax.all_gather(leaf_up, "leaf", axis=0, tiled=True)
    picked = jnp.take(shard_rows, my_far.reshape(-1), axis=0)
    picked = picked.reshape(leaf_rows, far_share, vector_count, rank_width)
    leaf_down_part = jnp.einsum(
        "ljkr,ljrs->lks", picked, far_blocks, preferred_element_type=jnp.float32
    )
    leaf_down_part = leaf_down_part.reshape(leaf_rows, flat_width)
    padded = with_halo(adjoint_in, (("leaf", 1),), REACH * panel_width)
    padded = padded.reshape(vector_count, leaf_rows + 2 * REACH, panel_width)
    my_near = lax.dynamic_slice_in_dim(near_sources, owner_index * near_share, near_share, 1)
    local_near = (my_near - first_leaf + REACH).reshape(-1)
    near_rows = jnp.take(padded, local_near, axis=1).reshape(
        vector_count, leaf_rows, near_share, panel_width
    )
    near_part = jnp.einsum(
        "kljp,ljpq->klq", near_rows, near_blocks, preferred_element_type=jnp.float32
    )
    near_part = near_part.reshape(vector_count, leaf_rows * panel_width)
    leaf_down, cluster_down, near_sum = (
        lax.psum_scatter(leaf_down_part, ("vec", "lvl"), scatter_dimension=1, tiled=True),
        lax.psum_scatter(cluster_part, ("vec", "lvl"), scatter_dimension=1, tiled=True),
        lax.psum_scatter(near_part, ("vec", "lvl"), scatter_dimension=0, tiled=True),
    )
    down_table = lax.all_gather(cluster_down.astype(jnp.bfloat16), "leaf", axis=0, tiled=True)
    pushed = jnp.take(down_table, parents, axis=0).reshape(leaf_rows, vector_share, rank_width)
    carried = jnp.einsum("lkc,lrc->lkr", pushed, col_transfer, preferred_element_type=jnp.float32)
    leaf_total = (leaf_down.reshape(leaf_rows, vector_share, rank_width) + carried).astype(
        jnp.bfloat16
    )
    far_out = jnp.einsum("lkr,lrp->klp", leaf_total, col_basis, preferred_element_type=jnp.float32)
    far_out = far_out.reshape(vector_share, leaf_rows * panel_width)
    return (far_out + near_sum).astype(jnp.bfloat16)


def up_kernel(x_hbm, basis_hbm, transfer_hbm, parents_hbm, coarse_hbm,
              msg_ref, short_ref, packed_ref,
              x_ref, basis_ref, transfer_ref, parents_ref, coarse_ref, sums, sems):
    copies = [
        pltpu.make_async_copy(a, b, sems.at[i])
        for i, (a, b) in enumerate((
            (x_hbm, x_ref),
            (basis_hbm, basis_ref),
            (parents_hbm, parents_ref),
            (transfer_hbm, transfer_ref),
            (coarse_hbm, coarse_ref),
        ))
    ]
    for copy in copies:
        copy.start()
    sums[...] = jnp.zeros_like(sums)
    leaves, rank, panel = basis_ref.shape
    z, c = lax.axis_index("leaf"), lax.axis_index("lvl")
    pairs = leaves // 2
    clusters = sums.shape[0]
    copies[0].wait()
    start = jnp.where((z + c) % 2 == 0, (leaves - REACH) * panel, 0)
    base = pairs + clusters // 2
    for i in range(REACH * panel // (2 * rank)):
        at = pl.multiple_of(start + i * 2 * rank, 2 * rank)
        msg_ref[base + i] = x_ref[:, pl.ds(at, 2 * rank)]
    copies[1].wait()
    ups = [
        dot_t(x_ref[:, l * panel:(l + 1) * panel], basis_ref[l]).astype(BF)
        for l in range(leaves)
    ]
    for p in range(pairs):
        msg_ref[p] = short_ref[p] = jnp.concatenate([ups[2 * p], ups[2 * p + 1]], axis=-1)
    copies[2].wait()
    copies[3].wait()
    branches = [dot(ups[l], transfer_ref[l]) for l in range(leaves)]
    for l in range(leaves):
        parent = parents_ref[l]
        sums[parent] = sums[parent] + branches[l]
    for p in range(clusters // 2):
        merged = jnp.concatenate([sums[2 * p], sums[2 * p + 1]], axis=-1).astype(BF)
        msg_ref[pairs + p] = short_ref[pairs + p] = merged
    copies[4].wait()
    for j in range(coarse_ref.shape[1]):
        packed_ref[j] = jnp.concatenate([coarse_ref[0, j], coarse_ref[1, j]], axis=-1)


def join_kernel(a_ref, b_ref, after_ref, out_ref):
    count = a_ref.shape[0]
    out_ref[:count] = a_ref[...]
    out_ref[count:] = b_ref[...]


def coarse_kernel(own_ref, a_ref, b_ref, other_ref, mix_ref, out_ref):
    clusters, rank, wide = mix_ref.shape
    count = a_ref.shape[0]
    lanes = []
    for q in range(b_ref.shape[0] - clusters // 2, b_ref.shape[0]):
        rest = b_ref[q].astype(F32) + other_ref[count + q].astype(F32)
        total = (own_ref[q].astype(F32) + a_ref[q].astype(F32)) + (
            other_ref[q].astype(F32) + rest
        )
        lanes.append(total.astype(BF))
    out_ref[...] = dot(
        jnp.concatenate(lanes, axis=-1), mix_ref[...].reshape(clusters * rank, wide)
    ).astype(BF)


def near_rows(sources, owner, z, l, leaves, share):
    return [sources[l, owner * share + j] - z * leaves + REACH for j in range(share)]


def mix_kernel(coarse_hbm, p_own, p_lvl, mix_ref, coarse_sources, sums, sem):
    copy = pltpu.make_async_copy(coarse_hbm, coarse_sources, sem)
    copy.start()
    share, rank, wide = p_own.shape
    owner = lax.axis_index("vec") * 2 + lax.axis_index("lvl")
    sums[...] = jnp.zeros_like(sums)
    low = low_half((rank, wide))
    copy.wait()
    for flip, blocks in ((0, p_own), (1, p_lvl)):
        base = (owner ^ flip) * share
        for j in range(share):
            block = blocks[j].astype(F32)
            for cluster, part in ((0, jnp.where(low, block, 0.0)), (1, jnp.where(low, 0.0, block))):
                source = coarse_sources[cluster, base + j]
                sums[source] = sums[source] + part
    mix_ref[...] = sums[...].astype(BF)


def prep_kernel(near_hbm, parents_hbm, x_ref, near_blocks_ref, transfer_ref, basis_ref,
                near_ref, weight_ref, near_sources, parents_ref, panels, sems):
    copies = [
        pltpu.make_async_copy(a, b, sems.at[i])
        for i, (a, b) in enumerate((
            (near_hbm, near_sources), (parents_hbm, parents_ref)
        ))
    ]
    for copy in copies:
        copy.start()
    leaves, share, panel, _ = near_blocks_ref.shape
    z, c = lax.axis_index("leaf"), lax.axis_index("lvl")
    owner = lax.axis_index("vec") * 2 + c
    weight_ref[...] = jnp.zeros_like(weight_ref)
    for l in range(leaves):
        panels[REACH + l] = x_ref[:, l * panel:(l + 1) * panel]
    weights = [
        lax.dot_general(
            transfer_ref[l], basis_ref[l], (((0,), (0,)), ((), ())), preferred_element_type=F32
        )
        for l in range(leaves)
    ]
    for copy in copies:
        copy.wait()
    for l in range(leaves):
        parent = parents_ref[l]
        distance = (parent >> 1) ^ z
        here = (distance & 1) == c
        slot = jnp.where(here, 2 * ((distance >> 1) ^ c) + (parent & 1), 0)
        weight_ref[l, slot] = jnp.where(here, weights[l], 0.0).astype(BF)
    for l in range(REACH, leaves - REACH):
        rows = [panels[i] for i in near_rows(near_sources, owner, z, l, leaves, share)]
        near_ref[l - REACH] = dot(
            jnp.concatenate(rows, axis=-1), near_blocks_ref[l].reshape(share * panel, panel)
        )


def local_kernel(near_hbm, far_hbm, own_ref, a_ref, b_ref, other_ref, x_ref,
                 near_blocks_ref, far_blocks_ref, basis_ref, near_ref, total_ref,
                 near_sources, far_sources, panels, table, sems):
    copies = [
        pltpu.make_async_copy(near_hbm, near_sources, sems.at[0]),
        pltpu.make_async_copy(far_hbm, far_sources, sems.at[1]),
    ]
    for copy in copies:
        copy.start()
    leaves, near_share, panel, _ = near_blocks_ref.shape
    far_share, rank = far_blocks_ref.shape[1:3]
    z, c = lax.axis_index("leaf"), lax.axis_index("lvl")
    owner = lax.axis_index("vec") * 2 + c
    high = (z + c) % 2 == 0
    top, bottom = leaves + REACH, 0
    at_mine = jnp.where(high, top, bottom)
    at_other = jnp.where(high, bottom, top)
    lanes = a_ref.shape[2]
    base = b_ref.shape[0]
    parts = panel // lanes
    count = a_ref.shape[0]
    for i in range(REACH):
        for w in range(parts):
            where = slice(w * lanes, (w + 1) * lanes)
            panels[at_mine + i, :, where] = a_ref[base + i * parts + w]
            panels[at_other + i, :, where] = other_ref[base + i * parts + w]
    for l in range(leaves):
        panels[REACH + l] = x_ref[:, l * panel:(l + 1) * panel]
    pairs = leaves // 2
    at_a = jnp.where(c == 1, 3, 1) * pairs
    at_o = jnp.where(c == 1, 1, 3) * pairs
    half = 4 * pairs
    for p in range(pairs):
        third = b_ref[p].astype(F32) + other_ref[count + p].astype(F32)
        for at, x in (
            (p, own_ref[p].astype(F32)),
            (2 * pairs + p, third),
            (at_a + p, a_ref[p].astype(F32)),
            (at_o + p, other_ref[p].astype(F32)),
        ):
            table[at] = x.astype(BF)
            table[half + at] = swap_halves(x).astype(BF)
    mask = z * leaves
    low = low_half((own_ref.shape[1], 2 * rank))
    for copy in copies:
        copy.wait()
    parts = []
    for l in range(leaves):
        rows = []
        for j in range(0, far_share, 2):
            s0 = far_sources[l, owner * far_share + j]
            s1 = far_sources[l, owner * far_share + j + 1]
            first = table[((s0 ^ mask) >> 1) + (s0 & 1) * half]
            second = table[((s1 ^ mask) >> 1) + half - (s1 & 1) * half]
            rows.append(jnp.where(low, first, second))
        parts.append(
            dot(jnp.concatenate(rows, axis=-1), far_blocks_ref[l].reshape(far_share * rank, rank))
        )
    for l in range(leaves):
        if REACH <= l < leaves - REACH:
            close = near_ref[l - REACH]
        else:
            rows = [
                panels[i] for i in near_rows(near_sources, owner, z, l, leaves, near_share)
            ]
            close = dot(
                jnp.concatenate(rows, axis=-1),
                near_blocks_ref[l].reshape(near_share * panel, panel),
            )
        total_ref[l] = close + dot(parts[l].astype(BF), basis_ref[l])


def down_kernel(total_ref, down_ref, first_ref, second_ref, weight_ref, send_ref, keep_ref):
    leaves, vectors, panel = total_ref.shape
    c = lax.axis_index("lvl")
    own, first, second = (r[...].astype(F32) for r in (down_ref, first_ref, second_ref))
    sources = jnp.concatenate(
        [jnp.where(c == 0, own, first), jnp.where(c == 0, first, second)], axis=-1
    ).astype(BF)
    rows = vectors // 4
    for l in range(leaves):
        part = total_ref[l] + dot(sources, weight_ref[l].reshape(sources.shape[1], panel))
        lanes = slice(l * panel, (l + 1) * panel)
        for w in range(2):
            even = part[2 * w * rows:(2 * w + 1) * rows]
            odd = part[(2 * w + 1) * rows:(2 * w + 2) * rows]
            keep_ref[w, :, lanes] = jnp.where(c == 0, even, odd)
            send_ref[w, :, lanes] = jnp.where(c == 0, odd, even).astype(BF)


def merge_kernel(keep_ref, got_ref, send_ref, rest_ref):
    v = lax.axis_index("vec")
    send_ref[...] = (keep_ref[1 - v] + got_ref[1 - v].astype(F32)).astype(BF)
    rest_ref[...] = keep_ref[v] + got_ref[v].astype(F32)


def in_hbm(*arrays):
    return [pltpu.with_memory_space_constraint(x, pltpu.HBM) for x in arrays]


def swap(x, route):
    axes = ("leaf", "vec", "lvl")
    zs, vs, cs = (lax.axis_size(a) for a in axes)
    pairs = []
    for z in range(zs):
        for v in range(vs):
            for c in range(cs):
                target = route(z, v, c)
                if target is not None:
                    tz, tv, tc = target
                    pairs.append(((z * vs + v) * cs + c, (tz * vs + tv) * cs + tc))
    return lax.ppermute(x, axes, pairs)


def on_device_paired(
    adjoint_in,
    row_basis,
    col_basis,
    row_transfer,
    col_transfer,
    parents,
    far_sources,
    far_blocks,
    coarse_sources,
    coarse_blocks,
    near_sources,
    near_blocks,
):
    vectors = adjoint_in.shape[0]
    leaves, rank, panel = row_basis.shape
    clusters = coarse_sources.shape[0] * 4
    width = leaves * panel
    params = pltpu.CompilerParams(vmem_limit_bytes=LIMIT)
    wide = 2 * rank
    messages = leaves // 2 + clusters // 2
    edges = REACH * panel // wide

    def other_core(z, v, c):
        return z, v, 1 - c

    def other_chip(z, v, c):
        return z, 1 - v, c

    msg, short, packed = pl.pallas_call(
        up_kernel,
        out_shape=(
            jax.ShapeDtypeStruct((messages + edges, vectors, wide), BF),
            jax.ShapeDtypeStruct((messages, vectors, wide), BF),
            jax.ShapeDtypeStruct((coarse_blocks.shape[1], rank, wide), BF),
        ),
        in_specs=[HBM] * 5,
        out_specs=(VMEM,) * 3,
        scratch_shapes=[
            pltpu.VMEM(adjoint_in.shape, BF),
            pltpu.VMEM(row_basis.shape, BF),
            pltpu.VMEM(row_transfer.shape, BF),
            pltpu.SMEM(parents.shape, jnp.int32),
            pltpu.VMEM(coarse_blocks.shape, BF),
            pltpu.VMEM((clusters, vectors, rank), F32),
            pltpu.SemaphoreType.DMA((5,)),
        ],
        compiler_params=params,
        cost_estimate=cost(1.5),
        name="up",
    )(*in_hbm(adjoint_in, row_basis, row_transfer, parents, coarse_blocks))
    a = swap(msg, lambda z, v, c: (z ^ (3 if c else 1), v, c))
    b = swap(short, lambda z, v, c: (z ^ 2, v, c) if c else None)
    p_lvl = swap(packed, other_core)
    near, weight = pl.pallas_call(
        prep_kernel,
        out_shape=(
            jax.ShapeDtypeStruct((leaves - 2 * REACH, vectors, panel), F32),
            jax.ShapeDtypeStruct((leaves, 4, rank, panel), BF),
        ),
        in_specs=[HBM] * 2 + [VMEM] * 4,
        out_specs=(VMEM,) * 2,
        scratch_shapes=[
            pltpu.SMEM(near_sources.shape, jnp.int32),
            pltpu.SMEM(parents.shape, jnp.int32),
            pltpu.VMEM((leaves + 2 * REACH, vectors, panel), BF),
            pltpu.SemaphoreType.DMA((2,)),
        ],
        compiler_params=params,
        cost_estimate=cost(1.5),
        name="prep",
    )(
        *in_hbm(near_sources, parents), adjoint_in, near_blocks, col_transfer, col_basis
    )
    mix = pl.pallas_call(
        mix_kernel,
        out_shape=jax.ShapeDtypeStruct((clusters, rank, wide), BF),
        in_specs=[HBM] + [VMEM] * 2,
        out_specs=VMEM,
        scratch_shapes=[
            pltpu.SMEM(coarse_sources.shape, jnp.int32),
            pltpu.VMEM((clusters, rank, wide), F32),
            pltpu.SemaphoreType.DMA(()),
        ],
        compiler_params=params,
        cost_estimate=cost(0.1),
        name="mix",
    )(*in_hbm(coarse_sources), packed, p_lvl)
    joined = pl.pallas_call(
        join_kernel,
        out_shape=jax.ShapeDtypeStruct((2 * messages + edges, vectors, wide), BF),
        in_specs=[VMEM] * 2 + [pl.BlockSpec(memory_space=pl.ANY)],
        out_specs=VMEM,
        compiler_params=params,
        cost_estimate=cost(0.5),
        name="join",
    )(a, b, mix)
    joined, near, weight = lax.optimization_barrier((joined, near, weight))
    other = swap(joined, other_core)
    down = pl.pallas_call(
        coarse_kernel,
        out_shape=jax.ShapeDtypeStruct((vectors, wide), BF),
        in_specs=[VMEM] * 5,
        out_specs=VMEM,
        compiler_params=params,
        cost_estimate=cost(0.5),
        name="coarse",
    )(msg, a, b, other, mix)
    first = swap(down, lambda z, v, c: (z ^ (3 if c else 2), v, c))
    second = swap(down, lambda z, v, c: (z ^ 1, v, c) if c else None)
    total = pl.pallas_call(
        local_kernel,
        out_shape=jax.ShapeDtypeStruct((leaves, vectors, panel), F32),
        in_specs=[HBM] * 2 + [VMEM] * 9,
        out_specs=VMEM,
        scratch_shapes=[
            pltpu.SMEM(near_sources.shape, jnp.int32),
            pltpu.SMEM(far_sources.shape, jnp.int32),
            pltpu.VMEM((leaves + 2 * REACH, vectors, panel), BF),
            pltpu.VMEM((4 * leaves, vectors, wide), BF),
            pltpu.SemaphoreType.DMA((2,)),
        ],
        compiler_params=params,
        cost_estimate=cost(4.0),
        name="local",
    )(
        near_sources, far_sources,
        msg, a, b, other, adjoint_in, near_blocks, far_blocks, col_basis, near,
    )
    rows = vectors // 4
    send, keep = pl.pallas_call(
        down_kernel,
        out_shape=(
            jax.ShapeDtypeStruct((2, rows, width), BF),
            jax.ShapeDtypeStruct((2, rows, width), F32),
        ),
        in_specs=[VMEM] * 5,
        out_specs=(VMEM,) * 2,
        compiler_params=params,
        cost_estimate=cost(1.0),
        name="down",
    )(total, down, first, second, weight)
    came = swap(send, other_core)
    send, rest = pl.pallas_call(
        merge_kernel,
        out_shape=(
            jax.ShapeDtypeStruct((rows, width), BF),
            jax.ShapeDtypeStruct((rows, width), F32),
        ),
        in_specs=[VMEM] * 2,
        out_specs=(VMEM,) * 2,
        compiler_params=params,
        cost_estimate=cost(0.6),
        name="merge",
    )(keep, came)
    came = swap(send, other_chip)
    return (rest + came.astype(F32)).astype(BF)


def solution(mesh):
    in_specs = (
        P("groups", "leaf"),
        P(("groups", "leaf"), None, None),
        P(("groups", "leaf"), None, None),
        P(("groups", "leaf"), None, None),
        P(("groups", "leaf"), None, None),
        P(("groups", "leaf")),
        P(("groups", "leaf"), None),
        P(("groups", "leaf"), ("vec", "lvl"), None, None),
        P(("groups", "leaf"), None),
        P(("groups", "leaf"), ("vec", "lvl"), None, None),
        P(("groups", "leaf"), None),
        P(("groups", "leaf"), ("vec", "lvl"), None, None),
    )
    out_specs = P(("groups", "vec", "lvl"), "leaf")
    sizes = tuple(mesh.shape[a] for a in ("leaf", "vec", "lvl"))
    body = on_device_paired if sizes == (4, 2, 2) else on_device_general
    return jax.shard_map(
        body, mesh=mesh, in_specs=in_specs, out_specs=out_specs, check_vma=False
    )
```

```python
import jax
import jax.numpy as jnp
from jax import lax
from jax.experimental import pallas as pl
from jax.experimental.pallas import tpu as pltpu
from jax.sharding import PartitionSpec as P

REACH = 2
BF = jnp.bfloat16
F32 = jnp.float32
VMEM = pl.BlockSpec(memory_space=pltpu.VMEM)
SMEM = pl.BlockSpec(memory_space=pltpu.SMEM)
HBM = pl.BlockSpec(memory_space=pltpu.HBM)
LIMIT = 32 << 20


def cost(us):
    return pl.CostEstimate(flops=int(us * 1e9), bytes_accessed=1024, transcendentals=0)


def dot(a, b):
    return jnp.dot(a, b, preferred_element_type=F32)


def dot_t(a, b):
    return lax.dot_general(a, b, (((1,), (1,)), ((), ())), preferred_element_type=F32)


def low_half(shape):
    return lax.broadcasted_iota(jnp.int32, shape, len(shape) - 1) < shape[-1] // 2


def swap_halves(x):
    half = x.shape[-1] // 2
    return jnp.concatenate([x[..., half:], x[..., :half]], axis=-1)


def with_halo(block, sides, width):
    for axis, dim in sides:
        count = lax.axis_size(axis)
        forward = [(i, i + 1) for i in range(count - 1)]
        backward = [(target, source) for source, target in forward]
        low = lax.ppermute(
            lax.slice_in_dim(block, block.shape[dim] - width, None, axis=dim), axis, forward
        )
        high = lax.ppermute(lax.slice_in_dim(block, 0, width, axis=dim), axis, backward)
        block = jnp.concatenate([low, block, high], axis=dim)
    return block


def on_device_general(
    adjoint_in,
    row_basis,
    col_basis,
    row_transfer,
    col_transfer,
    parents,
    far_sources,
    far_blocks,
    coarse_sources,
    coarse_blocks,
    near_sources,
    near_blocks,
):
    owner_count = lax.axis_size(("vec", "lvl"))
    owner_index = lax.axis_index(("vec", "lvl"))
    leaf_index = lax.axis_index("leaf")
    leaf_count = lax.axis_size("leaf")
    vector_count = adjoint_in.shape[0]
    leaf_rows, rank_width, panel_width = row_basis.shape
    cluster_rows = coarse_sources.shape[0]
    cluster_count = cluster_rows * leaf_count
    far_share = far_blocks.shape[1]
    coarse_share = coarse_blocks.shape[1]
    near_share = near_blocks.shape[1]
    vector_share = vector_count // owner_count
    first_leaf = leaf_index * leaf_rows
    flat_width = vector_count * rank_width
    x_blocks = adjoint_in.reshape(vector_count, leaf_rows, panel_width)
    leaf_up = jnp.einsum(
        "klp,lrp->lkr", x_blocks, row_basis, preferred_element_type=jnp.float32
    ).astype(jnp.bfloat16)
    branch = jnp.einsum("lkr,lrc->lkc", leaf_up, row_transfer, preferred_element_type=jnp.float32)
    branch_flat = branch.reshape(leaf_rows, flat_width)
    cluster_ids = lax.broadcasted_iota(jnp.int32, (cluster_count, leaf_rows), 0)
    members = (cluster_ids == parents[None, :]).astype(jnp.float32)
    partial_up = jnp.dot(members, branch_flat, precision=lax.Precision.HIGHEST)
    cluster_up = lax.psum(partial_up, "leaf").astype(jnp.bfloat16)
    cluster_up = cluster_up.reshape(cluster_count, vector_count, rank_width)
    my_coarse = lax.dynamic_slice_in_dim(
        coarse_sources, owner_index * coarse_share, coarse_share, 1
    )
    coarse_rows = jnp.take(cluster_up, my_coarse.reshape(-1), axis=0)
    coarse_rows = coarse_rows.reshape(cluster_rows, coarse_share, vector_count, rank_width)
    cluster_part = jnp.einsum(
        "cjkr,cjrs->cks", coarse_rows, coarse_blocks, preferred_element_type=jnp.float32
    )
    cluster_part = cluster_part.reshape(cluster_rows, flat_width)
    my_far = lax.dynamic_slice_in_dim(far_sources, owner_index * far_share, far_share, 1)
    shard_rows = lax.all_gather(leaf_up, "leaf", axis=0, tiled=True)
    picked = jnp.take(shard_rows, my_far.reshape(-1), axis=0)
    picked = picked.reshape(leaf_rows, far_share, vector_count, rank_width)
    leaf_down_part = jnp.einsum(
        "ljkr,ljrs->lks", picked, far_blocks, preferred_element_type=jnp.float32
    )
    leaf_down_part = leaf_down_part.reshape(leaf_rows, flat_width)
    padded = with_halo(adjoint_in, (("leaf", 1),), REACH * panel_width)
    padded = padded.reshape(vector_count, leaf_rows + 2 * REACH, panel_width)
    my_near = lax.dynamic_slice_in_dim(near_sources, owner_index * near_share, near_share, 1)
    local_near = (my_near - first_leaf + REACH).reshape(-1)
    near_rows = jnp.take(padded, local_near, axis=1).reshape(
        vector_count, leaf_rows, near_share, panel_width
    )
    near_part = jnp.einsum(
        "kljp,ljpq->klq", near_rows, near_blocks, preferred_element_type=jnp.float32
    )
    near_part = near_part.reshape(vector_count, leaf_rows * panel_width)
    leaf_down, cluster_down, near_sum = (
        lax.psum_scatter(leaf_down_part, ("vec", "lvl"), scatter_dimension=1, tiled=True),
        lax.psum_scatter(cluster_part, ("vec", "lvl"), scatter_dimension=1, tiled=True),
        lax.psum_scatter(near_part, ("vec", "lvl"), scatter_dimension=0, tiled=True),
    )
    down_table = lax.all_gather(cluster_down.astype(jnp.bfloat16), "leaf", axis=0, tiled=True)
    pushed = jnp.take(down_table, parents, axis=0).reshape(leaf_rows, vector_share, rank_width)
    carried = jnp.einsum("lkc,lrc->lkr", pushed, col_transfer, preferred_element_type=jnp.float32)
    leaf_total = (leaf_down.reshape(leaf_rows, vector_share, rank_width) + carried).astype(
        jnp.bfloat16
    )
    far_out = jnp.einsum("lkr,lrp->klp", leaf_total, col_basis, preferred_element_type=jnp.float32)
    far_out = far_out.reshape(vector_share, leaf_rows * panel_width)
    return (far_out + near_sum).astype(jnp.bfloat16)


def up_kernel(x_hbm, basis_hbm, transfer_hbm, parents_hbm, coarse_hbm,
              msg_ref, short_ref, packed_ref,
              x_ref, basis_ref, transfer_ref, parents_ref, coarse_ref, sums, sems):
    copies = [
        pltpu.make_async_copy(a, b, sems.at[i])
        for i, (a, b) in enumerate((
            (x_hbm, x_ref),
            (basis_hbm, basis_ref),
            (parents_hbm, parents_ref),
            (transfer_hbm, transfer_ref),
            (coarse_hbm, coarse_ref),
        ))
    ]
    for copy in copies:
        copy.start()
    sums[...] = jnp.zeros_like(sums)
    leaves, rank, panel = basis_ref.shape
    z, c = lax.axis_index("leaf"), lax.axis_index("lvl")
    pairs = leaves // 2
    clusters = sums.shape[0]
    copies[0].wait()
    start = jnp.where((z + c) % 2 == 0, (leaves - REACH) * panel, 0)
    base = pairs + clusters // 2
    for i in range(REACH * panel // (2 * rank)):
        at = pl.multiple_of(start + i * 2 * rank, 2 * rank)
        msg_ref[base + i] = x_ref[:, pl.ds(at, 2 * rank)]
    copies[1].wait()
    ups = [
        dot_t(x_ref[:, l * panel:(l + 1) * panel], basis_ref[l]).astype(BF)
        for l in range(leaves)
    ]
    for p in range(pairs):
        msg_ref[p] = short_ref[p] = jnp.concatenate([ups[2 * p], ups[2 * p + 1]], axis=-1)
    copies[2].wait()
    copies[3].wait()
    branches = [dot(ups[l], transfer_ref[l]) for l in range(leaves)]
    for l in range(leaves):
        parent = parents_ref[l]
        sums[parent] = sums[parent] + branches[l]
    for p in range(clusters // 2):
        merged = jnp.concatenate([sums[2 * p], sums[2 * p + 1]], axis=-1).astype(BF)
        msg_ref[pairs + p] = short_ref[pairs + p] = merged
    copies[4].wait()
    for j in range(coarse_ref.shape[1]):
        packed_ref[j] = jnp.concatenate([coarse_ref[0, j], coarse_ref[1, j]], axis=-1)


def coarse_kernel(*refs):
    pieces, (mix_ref, out_ref) = refs[:-2], refs[-2:]
    clusters, rank, wide = mix_ref.shape
    first = clusters // 2
    lanes = []
    for q in range(first, 2 * first):
        total = pieces[0][q].astype(F32)
        for piece in pieces[1:]:
            total = total + piece[q].astype(F32)
        lanes.append(total.astype(BF))
    out_ref[...] = dot(
        jnp.concatenate(lanes, axis=-1), mix_ref[...].reshape(clusters * rank, wide)
    ).astype(BF)


def near_rows(sources, owner, z, l, leaves, share):
    return [sources[l, owner * share + j] - z * leaves + REACH for j in range(share)]


def mix_kernel(coarse_hbm, p_own, p_lvl, mix_ref, coarse_sources, sums, sem):
    copy = pltpu.make_async_copy(coarse_hbm, coarse_sources, sem)
    copy.start()
    share, rank, wide = p_own.shape
    owner = lax.axis_index("vec") * 2 + lax.axis_index("lvl")
    sums[...] = jnp.zeros_like(sums)
    low = low_half((rank, wide))
    copy.wait()
    for flip, blocks in ((0, p_own), (1, p_lvl)):
        base = (owner ^ flip) * share
        for j in range(share):
            block = blocks[j].astype(F32)
            for cluster, part in ((0, jnp.where(low, block, 0.0)), (1, jnp.where(low, 0.0, block))):
                source = coarse_sources[cluster, base + j]
                sums[source] = sums[source] + part
    mix_ref[...] = sums[...].astype(BF)


def prep_kernel(near_hbm, parents_hbm, x_ref, near_blocks_ref, transfer_ref, basis_ref,
                near_ref, weight_ref, near_sources, parents_ref, panels, sems):
    copies = [
        pltpu.make_async_copy(a, b, sems.at[i])
        for i, (a, b) in enumerate((
            (near_hbm, near_sources), (parents_hbm, parents_ref)
        ))
    ]
    for copy in copies:
        copy.start()
    leaves, share, panel, _ = near_blocks_ref.shape
    z, c = lax.axis_index("leaf"), lax.axis_index("lvl")
    owner = lax.axis_index("vec") * 2 + c
    weight_ref[...] = jnp.zeros_like(weight_ref)
    for l in range(leaves):
        panels[REACH + l] = x_ref[:, l * panel:(l + 1) * panel]
    weights = [
        lax.dot_general(
            transfer_ref[l], basis_ref[l], (((0,), (0,)), ((), ())), preferred_element_type=F32
        )
        for l in range(leaves)
    ]
    for copy in copies:
        copy.wait()
    for l in range(leaves):
        parent = parents_ref[l]
        distance = (parent >> 1) ^ z
        here = ((distance ^ (distance >> 1)) & 1) == c
        slot = jnp.where(here, 2 * (distance >> 1) + (parent & 1), 0)
        weight_ref[l, slot] = jnp.where(here, weights[l], 0.0).astype(BF)
    for l in range(REACH, leaves - REACH):
        rows = [panels[i] for i in near_rows(near_sources, owner, z, l, leaves, share)]
        near_ref[l - REACH] = dot(
            jnp.concatenate(rows, axis=-1), near_blocks_ref[l].reshape(share * panel, panel)
        )


def local_kernel(near_hbm, far_hbm, own_ref, a_ref, b_ref, la_ref, lb_ref, x_ref,
                 near_blocks_ref, far_blocks_ref, basis_ref, near_ref, total_ref,
                 near_sources, far_sources, panels, table, sems):
    copies = [
        pltpu.make_async_copy(near_hbm, near_sources, sems.at[0]),
        pltpu.make_async_copy(far_hbm, far_sources, sems.at[1]),
    ]
    for copy in copies:
        copy.start()
    leaves, near_share, panel, _ = near_blocks_ref.shape
    far_share, rank = far_blocks_ref.shape[1:3]
    z, c = lax.axis_index("leaf"), lax.axis_index("lvl")
    owner = lax.axis_index("vec") * 2 + c
    high = (z + c) % 2 == 0
    top, bottom = leaves + REACH, 0
    at_mine = jnp.where(high, top, bottom)
    at_other = jnp.where(high, bottom, top)
    lanes = a_ref.shape[2]
    base = b_ref.shape[0]
    parts = panel // lanes
    for i in range(REACH):
        for w in range(parts):
            where = slice(w * lanes, (w + 1) * lanes)
            panels[at_mine + i, :, where] = a_ref[base + i * parts + w]
            panels[at_other + i, :, where] = la_ref[base + i * parts + w]
    for l in range(leaves):
        panels[REACH + l] = x_ref[:, l * panel:(l + 1) * panel]
    pairs = leaves // 2
    at_a = jnp.where(c == 1, 3, 1) * pairs
    at_o = jnp.where(c == 1, 1, 3) * pairs
    half = 4 * pairs
    for p in range(pairs):
        third = b_ref[p].astype(F32) + lb_ref[p].astype(F32)
        for at, x in (
            (p, own_ref[p].astype(F32)),
            (2 * pairs + p, third),
            (at_a + p, a_ref[p].astype(F32)),
            (at_o + p, la_ref[p].astype(F32)),
        ):
            table[at] = x.astype(BF)
            table[half + at] = swap_halves(x).astype(BF)
    mask = z * leaves
    low = low_half((own_ref.shape[1], 2 * rank))
    for copy in copies:
        copy.wait()
    parts = []
    for l in range(leaves):
        rows = []
        for j in range(0, far_share, 2):
            s0 = far_sources[l, owner * far_share + j]
            s1 = far_sources[l, owner * far_share + j + 1]
            first = table[((s0 ^ mask) >> 1) + (s0 & 1) * half]
            second = table[((s1 ^ mask) >> 1) + half - (s1 & 1) * half]
            rows.append(jnp.where(low, first, second))
        parts.append(
            dot(jnp.concatenate(rows, axis=-1), far_blocks_ref[l].reshape(far_share * rank, rank))
        )
    for l in range(leaves):
        if REACH <= l < leaves - REACH:
            close = near_ref[l - REACH]
        else:
            rows = [
                panels[i] for i in near_rows(near_sources, owner, z, l, leaves, near_share)
            ]
            close = dot(
                jnp.concatenate(rows, axis=-1),
                near_blocks_ref[l].reshape(near_share * panel, panel),
            )
        total_ref[l] = close + dot(parts[l].astype(BF), basis_ref[l])


def down_kernel(total_ref, down_ref, first_ref, second_ref, weight_ref, send_ref, keep_ref):
    leaves, vectors, panel = total_ref.shape
    c = lax.axis_index("lvl")
    own, first, second = (r[...].astype(F32) for r in (down_ref, first_ref, second_ref))
    sources = jnp.concatenate(
        [jnp.where(c == 0, own, first), jnp.where(c == 0, first, second)], axis=-1
    ).astype(BF)
    rows = vectors // 4
    for l in range(leaves):
        part = total_ref[l] + dot(sources, weight_ref[l].reshape(sources.shape[1], panel))
        lanes = slice(l * panel, (l + 1) * panel)
        for w in range(2):
            even = part[2 * w * rows:(2 * w + 1) * rows]
            odd = part[(2 * w + 1) * rows:(2 * w + 2) * rows]
            keep_ref[w, :, lanes] = jnp.where(c == 0, even, odd)
            send_ref[w, :, lanes] = jnp.where(c == 0, odd, even).astype(BF)


def merge_kernel(keep_ref, got_ref, send_ref, rest_ref):
    v = lax.axis_index("vec")
    send_ref[...] = (keep_ref[1 - v] + got_ref[1 - v].astype(F32)).astype(BF)
    rest_ref[...] = keep_ref[v] + got_ref[v].astype(F32)


def in_hbm(*arrays):
    return [pltpu.with_memory_space_constraint(x, pltpu.HBM) for x in arrays]


def swap(x, route):
    axes = ("leaf", "vec", "lvl")
    zs, vs, cs = (lax.axis_size(a) for a in axes)
    pairs = []
    for z in range(zs):
        for v in range(vs):
            for c in range(cs):
                target = route(z, v, c)
                if target is not None:
                    tz, tv, tc = target
                    pairs.append(((z * vs + v) * cs + c, (tz * vs + tv) * cs + tc))
    return lax.ppermute(x, axes, pairs)


def on_device_paired(
    adjoint_in,
    row_basis,
    col_basis,
    row_transfer,
    col_transfer,
    parents,
    far_sources,
    far_blocks,
    coarse_sources,
    coarse_blocks,
    near_sources,
    near_blocks,
):
    vectors = adjoint_in.shape[0]
    leaves, rank, panel = row_basis.shape
    clusters = coarse_sources.shape[0] * 4
    width = leaves * panel
    params = pltpu.CompilerParams(vmem_limit_bytes=LIMIT)
    wide = 2 * rank
    messages = leaves // 2 + clusters // 2
    edges = REACH * panel // wide

    def other_core(z, v, c):
        return z, v, 1 - c

    def other_chip(z, v, c):
        return z, 1 - v, c

    msg, short, packed = pl.pallas_call(
        up_kernel,
        out_shape=(
            jax.ShapeDtypeStruct((messages + edges, vectors, wide), BF),
            jax.ShapeDtypeStruct((messages, vectors, wide), BF),
            jax.ShapeDtypeStruct((coarse_blocks.shape[1], rank, wide), BF),
        ),
        in_specs=[HBM] * 5,
        out_specs=(VMEM,) * 3,
        scratch_shapes=[
            pltpu.VMEM(adjoint_in.shape, BF),
            pltpu.VMEM(row_basis.shape, BF),
            pltpu.VMEM(row_transfer.shape, BF),
            pltpu.SMEM(parents.shape, jnp.int32),
            pltpu.VMEM(coarse_blocks.shape, BF),
            pltpu.VMEM((clusters, vectors, rank), F32),
            pltpu.SemaphoreType.DMA((5,)),
        ],
        compiler_params=params,
        cost_estimate=cost(1.5),
        name="up",
    )(*in_hbm(adjoint_in, row_basis, row_transfer, parents, coarse_blocks))
    a = swap(msg, lambda z, v, c: (z ^ (3 if c else 1), v, c))
    b = swap(short, lambda z, v, c: (z ^ 2, v, c) if c else None)
    p_lvl = swap(packed, other_core)
    near, weight = pl.pallas_call(
        prep_kernel,
        out_shape=(
            jax.ShapeDtypeStruct((leaves - 2 * REACH, vectors, panel), F32),
            jax.ShapeDtypeStruct((leaves, 4, rank, panel), BF),
        ),
        in_specs=[HBM] * 2 + [VMEM] * 4,
        out_specs=(VMEM,) * 2,
        scratch_shapes=[
            pltpu.SMEM(near_sources.shape, jnp.int32),
            pltpu.SMEM(parents.shape, jnp.int32),
            pltpu.VMEM((leaves + 2 * REACH, vectors, panel), BF),
            pltpu.SemaphoreType.DMA((2,)),
        ],
        compiler_params=params,
        cost_estimate=cost(1.5),
        name="prep",
    )(
        *in_hbm(near_sources, parents), adjoint_in, near_blocks, col_transfer, col_basis
    )
    mix = pl.pallas_call(
        mix_kernel,
        out_shape=jax.ShapeDtypeStruct((clusters, rank, wide), BF),
        in_specs=[HBM] + [VMEM] * 2,
        out_specs=VMEM,
        scratch_shapes=[
            pltpu.SMEM(coarse_sources.shape, jnp.int32),
            pltpu.VMEM((clusters, rank, wide), F32),
            pltpu.SemaphoreType.DMA(()),
        ],
        compiler_params=params,
        cost_estimate=cost(0.1),
        name="mix",
    )(*in_hbm(coarse_sources), packed, p_lvl)
    a, near, weight, mix = lax.optimization_barrier((a, near, weight, mix))
    la = swap(a, other_core)
    lb = swap(b, other_core)

    def coarse(*pieces):
        return pl.pallas_call(
            coarse_kernel,
            out_shape=jax.ShapeDtypeStruct((vectors, wide), BF),
            in_specs=[VMEM] * (len(pieces) + 1),
            out_specs=VMEM,
            compiler_params=params,
            cost_estimate=cost(0.2),
            name="coarse",
        )(*pieces, mix)

    down = coarse(msg, a, la, b, lb)
    first = swap(down, lambda z, v, c: (z ^ (1 if c else 3), v, c))
    second = swap(down, lambda z, v, c: (z ^ 2, v, c) if c else None)
    total = pl.pallas_call(
        local_kernel,
        out_shape=jax.ShapeDtypeStruct((leaves, vectors, panel), F32),
        in_specs=[HBM] * 2 + [VMEM] * 10,
        out_specs=VMEM,
        scratch_shapes=[
            pltpu.SMEM(near_sources.shape, jnp.int32),
            pltpu.SMEM(far_sources.shape, jnp.int32),
            pltpu.VMEM((leaves + 2 * REACH, vectors, panel), BF),
            pltpu.VMEM((4 * leaves, vectors, wide), BF),
            pltpu.SemaphoreType.DMA((2,)),
        ],
        compiler_params=params,
        cost_estimate=cost(4.0),
        name="local",
    )(
        near_sources, far_sources,
        msg, a, b, la, lb, adjoint_in, near_blocks, far_blocks, col_basis, near,
    )
    rows = vectors // 4
    send, keep = pl.pallas_call(
        down_kernel,
        out_shape=(
            jax.ShapeDtypeStruct((2, rows, width), BF),
            jax.ShapeDtypeStruct((2, rows, width), F32),
        ),
        in_specs=[VMEM] * 5,
        out_specs=(VMEM,) * 2,
        compiler_params=params,
        cost_estimate=cost(1.0),
        name="down",
    )(total, down, first, second, weight)
    came = swap(send, other_core)
    send, rest = pl.pallas_call(
        merge_kernel,
        out_shape=(
            jax.ShapeDtypeStruct((rows, width), BF),
            jax.ShapeDtypeStruct((rows, width), F32),
        ),
        in_specs=[VMEM] * 2,
        out_specs=(VMEM,) * 2,
        compiler_params=params,
        cost_estimate=cost(0.6),
        name="merge",
    )(keep, came)
    came = swap(send, other_chip)
    return (rest + came.astype(F32)).astype(BF)


def solution(mesh):
    in_specs = (
        P("groups", "leaf"),
        P(("groups", "leaf"), None, None),
        P(("groups", "leaf"), None, None),
        P(("groups", "leaf"), None, None),
        P(("groups", "leaf"), None, None),
        P(("groups", "leaf")),
        P(("groups", "leaf"), None),
        P(("groups", "leaf"), ("vec", "lvl"), None, None),
        P(("groups", "leaf"), None),
        P(("groups", "leaf"), ("vec", "lvl"), None, None),
        P(("groups", "leaf"), None),
        P(("groups", "leaf"), ("vec", "lvl"), None, None),
    )
    out_specs = P(("groups", "vec", "lvl"), "leaf")
    sizes = tuple(mesh.shape[a] for a in ("leaf", "vec", "lvl"))
    body = on_device_paired if sizes == (4, 2, 2) else on_device_general
    return jax.shard_map(
        body, mesh=mesh, in_specs=in_specs, out_specs=out_specs, check_vma=False
    )
```

```python
import jax
import jax.numpy as jnp
from jax import lax
from jax.experimental import pallas as pl
from jax.experimental.pallas import tpu as pltpu
from jax.sharding import PartitionSpec as P

REACH = 2
BF = jnp.bfloat16
F32 = jnp.float32
VMEM = pl.BlockSpec(memory_space=pltpu.VMEM)
SMEM = pl.BlockSpec(memory_space=pltpu.SMEM)
HBM = pl.BlockSpec(memory_space=pltpu.HBM)
LIMIT = 32 << 20


def cost(us):
    return pl.CostEstimate(flops=int(us * 1e9), bytes_accessed=1024, transcendentals=0)


def dot(a, b):
    return jnp.dot(a, b, preferred_element_type=F32)


def dot_t(a, b):
    return lax.dot_general(a, b, (((1,), (1,)), ((), ())), preferred_element_type=F32)


def low_half(shape):
    return lax.broadcasted_iota(jnp.int32, shape, len(shape) - 1) < shape[-1] // 2


def swap_halves(x):
    half = x.shape[-1] // 2
    return jnp.concatenate([x[..., half:], x[..., :half]], axis=-1)


def with_halo(block, sides, width):
    for axis, dim in sides:
        count = lax.axis_size(axis)
        forward = [(i, i + 1) for i in range(count - 1)]
        backward = [(target, source) for source, target in forward]
        low = lax.ppermute(
            lax.slice_in_dim(block, block.shape[dim] - width, None, axis=dim), axis, forward
        )
        high = lax.ppermute(lax.slice_in_dim(block, 0, width, axis=dim), axis, backward)
        block = jnp.concatenate([low, block, high], axis=dim)
    return block


def on_device_general(
    adjoint_in,
    row_basis,
    col_basis,
    row_transfer,
    col_transfer,
    parents,
    far_sources,
    far_blocks,
    coarse_sources,
    coarse_blocks,
    near_sources,
    near_blocks,
):
    owner_count = lax.axis_size(("vec", "lvl"))
    owner_index = lax.axis_index(("vec", "lvl"))
    leaf_index = lax.axis_index("leaf")
    leaf_count = lax.axis_size("leaf")
    vector_count = adjoint_in.shape[0]
    leaf_rows, rank_width, panel_width = row_basis.shape
    cluster_rows = coarse_sources.shape[0]
    cluster_count = cluster_rows * leaf_count
    far_share = far_blocks.shape[1]
    coarse_share = coarse_blocks.shape[1]
    near_share = near_blocks.shape[1]
    vector_share = vector_count // owner_count
    first_leaf = leaf_index * leaf_rows
    flat_width = vector_count * rank_width
    x_blocks = adjoint_in.reshape(vector_count, leaf_rows, panel_width)
    leaf_up = jnp.einsum(
        "klp,lrp->lkr", x_blocks, row_basis, preferred_element_type=jnp.float32
    ).astype(jnp.bfloat16)
    branch = jnp.einsum("lkr,lrc->lkc", leaf_up, row_transfer, preferred_element_type=jnp.float32)
    branch_flat = branch.reshape(leaf_rows, flat_width)
    cluster_ids = lax.broadcasted_iota(jnp.int32, (cluster_count, leaf_rows), 0)
    members = (cluster_ids == parents[None, :]).astype(jnp.float32)
    partial_up = jnp.dot(members, branch_flat, precision=lax.Precision.HIGHEST)
    cluster_up = lax.psum(partial_up, "leaf").astype(jnp.bfloat16)
    cluster_up = cluster_up.reshape(cluster_count, vector_count, rank_width)
    my_coarse = lax.dynamic_slice_in_dim(
        coarse_sources, owner_index * coarse_share, coarse_share, 1
    )
    coarse_rows = jnp.take(cluster_up, my_coarse.reshape(-1), axis=0)
    coarse_rows = coarse_rows.reshape(cluster_rows, coarse_share, vector_count, rank_width)
    cluster_part = jnp.einsum(
        "cjkr,cjrs->cks", coarse_rows, coarse_blocks, preferred_element_type=jnp.float32
    )
    cluster_part = cluster_part.reshape(cluster_rows, flat_width)
    my_far = lax.dynamic_slice_in_dim(far_sources, owner_index * far_share, far_share, 1)
    shard_rows = lax.all_gather(leaf_up, "leaf", axis=0, tiled=True)
    picked = jnp.take(shard_rows, my_far.reshape(-1), axis=0)
    picked = picked.reshape(leaf_rows, far_share, vector_count, rank_width)
    leaf_down_part = jnp.einsum(
        "ljkr,ljrs->lks", picked, far_blocks, preferred_element_type=jnp.float32
    )
    leaf_down_part = leaf_down_part.reshape(leaf_rows, flat_width)
    padded = with_halo(adjoint_in, (("leaf", 1),), REACH * panel_width)
    padded = padded.reshape(vector_count, leaf_rows + 2 * REACH, panel_width)
    my_near = lax.dynamic_slice_in_dim(near_sources, owner_index * near_share, near_share, 1)
    local_near = (my_near - first_leaf + REACH).reshape(-1)
    near_rows = jnp.take(padded, local_near, axis=1).reshape(
        vector_count, leaf_rows, near_share, panel_width
    )
    near_part = jnp.einsum(
        "kljp,ljpq->klq", near_rows, near_blocks, preferred_element_type=jnp.float32
    )
    near_part = near_part.reshape(vector_count, leaf_rows * panel_width)
    leaf_down, cluster_down, near_sum = (
        lax.psum_scatter(leaf_down_part, ("vec", "lvl"), scatter_dimension=1, tiled=True),
        lax.psum_scatter(cluster_part, ("vec", "lvl"), scatter_dimension=1, tiled=True),
        lax.psum_scatter(near_part, ("vec", "lvl"), scatter_dimension=0, tiled=True),
    )
    down_table = lax.all_gather(cluster_down.astype(jnp.bfloat16), "leaf", axis=0, tiled=True)
    pushed = jnp.take(down_table, parents, axis=0).reshape(leaf_rows, vector_share, rank_width)
    carried = jnp.einsum("lkc,lrc->lkr", pushed, col_transfer, preferred_element_type=jnp.float32)
    leaf_total = (leaf_down.reshape(leaf_rows, vector_share, rank_width) + carried).astype(
        jnp.bfloat16
    )
    far_out = jnp.einsum("lkr,lrp->klp", leaf_total, col_basis, preferred_element_type=jnp.float32)
    far_out = far_out.reshape(vector_share, leaf_rows * panel_width)
    return (far_out + near_sum).astype(jnp.bfloat16)


def up_kernel(x_hbm, basis_hbm, transfer_hbm, parents_hbm, coarse_hbm,
              msg_ref, short_ref, packed_ref,
              x_ref, basis_ref, transfer_ref, parents_ref, coarse_ref, sums, sems):
    copies = [
        pltpu.make_async_copy(a, b, sems.at[i])
        for i, (a, b) in enumerate((
            (x_hbm, x_ref),
            (basis_hbm, basis_ref),
            (parents_hbm, parents_ref),
            (transfer_hbm, transfer_ref),
            (coarse_hbm, coarse_ref),
        ))
    ]
    for copy in copies:
        copy.start()
    sums[...] = jnp.zeros_like(sums)
    leaves, rank, panel = basis_ref.shape
    z, c = lax.axis_index("leaf"), lax.axis_index("lvl")
    pairs = leaves // 2
    clusters = sums.shape[0]
    copies[0].wait()
    start = jnp.where((z + c) % 2 == 0, (leaves - REACH) * panel, 0)
    base = pairs + clusters // 2
    for i in range(REACH * panel // (2 * rank)):
        at = pl.multiple_of(start + i * 2 * rank, 2 * rank)
        msg_ref[base + i] = x_ref[:, pl.ds(at, 2 * rank)]
    copies[1].wait()
    ups = [
        dot_t(x_ref[:, l * panel:(l + 1) * panel], basis_ref[l]).astype(BF)
        for l in range(leaves)
    ]
    for p in range(pairs):
        msg_ref[p] = short_ref[p] = jnp.concatenate([ups[2 * p], ups[2 * p + 1]], axis=-1)
    copies[2].wait()
    copies[3].wait()
    branches = [dot(ups[l], transfer_ref[l]) for l in range(leaves)]
    for l in range(leaves):
        parent = parents_ref[l]
        sums[parent] = sums[parent] + branches[l]
    for p in range(clusters // 2):
        merged = jnp.concatenate([sums[2 * p], sums[2 * p + 1]], axis=-1).astype(BF)
        msg_ref[pairs + p] = short_ref[pairs + p] = merged
    copies[4].wait()
    for j in range(coarse_ref.shape[1]):
        packed_ref[j] = jnp.concatenate([coarse_ref[0, j], coarse_ref[1, j]], axis=-1)


def coarse_kernel(*refs):
    pieces, (mix_ref, out_ref) = refs[:-2], refs[-2:]
    clusters, rank, wide = mix_ref.shape
    first = clusters // 2
    lanes = []
    for q in range(first, 2 * first):
        total = pieces[0][q].astype(F32)
        for piece in pieces[1:]:
            total = total + piece[q].astype(F32)
        lanes.append(total.astype(BF))
    out_ref[...] = dot(
        jnp.concatenate(lanes, axis=-1), mix_ref[...].reshape(clusters * rank, wide)
    ).astype(BF)


def near_rows(sources, owner, z, l, leaves, share):
    return [sources[l, owner * share + j] - z * leaves + REACH for j in range(share)]


def mix_kernel(coarse_hbm, p_own, p_lvl, mix_ref, coarse_sources, sums, sem):
    copy = pltpu.make_async_copy(coarse_hbm, coarse_sources, sem)
    copy.start()
    share, rank, wide = p_own.shape
    owner = lax.axis_index("vec") * 2 + lax.axis_index("lvl")
    sums[...] = jnp.zeros_like(sums)
    low = low_half((rank, wide))
    copy.wait()
    for flip, blocks in ((0, p_own), (1, p_lvl)):
        base = (owner ^ flip) * share
        for j in range(share):
            block = blocks[j].astype(F32)
            for cluster, part in ((0, jnp.where(low, block, 0.0)), (1, jnp.where(low, 0.0, block))):
                source = coarse_sources[cluster, base + j]
                sums[source] = sums[source] + part
    mix_ref[...] = sums[...].astype(BF)


def prep_kernel(near_hbm, parents_hbm, x_ref, near_blocks_ref, transfer_ref, basis_ref,
                near_ref, weight_ref, near_sources, parents_ref, panels, sems):
    copies = [
        pltpu.make_async_copy(a, b, sems.at[i])
        for i, (a, b) in enumerate((
            (near_hbm, near_sources), (parents_hbm, parents_ref)
        ))
    ]
    for copy in copies:
        copy.start()
    leaves, share, panel, _ = near_blocks_ref.shape
    z, c = lax.axis_index("leaf"), lax.axis_index("lvl")
    owner = lax.axis_index("vec") * 2 + c
    weight_ref[...] = jnp.zeros_like(weight_ref)
    for l in range(leaves):
        panels[REACH + l] = x_ref[:, l * panel:(l + 1) * panel]
    weights = [
        lax.dot_general(
            transfer_ref[l], basis_ref[l], (((0,), (0,)), ((), ())), preferred_element_type=F32
        )
        for l in range(leaves)
    ]
    for copy in copies:
        copy.wait()
    for l in range(leaves):
        parent = parents_ref[l]
        distance = (parent >> 1) ^ z
        here = ((distance ^ (distance >> 1)) & 1) == c
        slot = jnp.where(here, 2 * (distance >> 1) + (parent & 1), 0)
        weight_ref[l, slot] = jnp.where(here, weights[l], 0.0).astype(BF)
    for l in range(REACH, leaves - REACH):
        rows = [panels[i] for i in near_rows(near_sources, owner, z, l, leaves, share)]
        near_ref[l - REACH] = dot(
            jnp.concatenate(rows, axis=-1), near_blocks_ref[l].reshape(share * panel, panel)
        )


def local_kernel(near_hbm, far_hbm, own_ref, a_ref, b_ref, la_ref, lb_ref, x_ref,
                 near_blocks_ref, far_blocks_ref, basis_ref, near_ref, total_ref,
                 near_sources, far_sources, panels, table, sems):
    copies = [
        pltpu.make_async_copy(near_hbm, near_sources, sems.at[0]),
        pltpu.make_async_copy(far_hbm, far_sources, sems.at[1]),
    ]
    for copy in copies:
        copy.start()
    leaves, near_share, panel, _ = near_blocks_ref.shape
    far_share, rank = far_blocks_ref.shape[1:3]
    z, c = lax.axis_index("leaf"), lax.axis_index("lvl")
    owner = lax.axis_index("vec") * 2 + c
    high = (z + c) % 2 == 0
    top, bottom = leaves + REACH, 0
    at_mine = jnp.where(high, top, bottom)
    at_other = jnp.where(high, bottom, top)
    lanes = a_ref.shape[2]
    base = b_ref.shape[0]
    parts = panel // lanes
    for i in range(REACH):
        for w in range(parts):
            where = slice(w * lanes, (w + 1) * lanes)
            panels[at_mine + i, :, where] = a_ref[base + i * parts + w]
            panels[at_other + i, :, where] = la_ref[base + i * parts + w]
    for l in range(leaves):
        panels[REACH + l] = x_ref[:, l * panel:(l + 1) * panel]
    pairs = leaves // 2
    at_a = jnp.where(c == 1, 3, 1) * pairs
    at_o = jnp.where(c == 1, 1, 3) * pairs
    half = 4 * pairs
    for p in range(pairs):
        third = b_ref[p].astype(F32) + lb_ref[p].astype(F32)
        for at, x in (
            (p, own_ref[p].astype(F32)),
            (2 * pairs + p, third),
            (at_a + p, a_ref[p].astype(F32)),
            (at_o + p, la_ref[p].astype(F32)),
        ):
            table[at] = x.astype(BF)
            table[half + at] = swap_halves(x).astype(BF)
    mask = z * leaves
    low = low_half((own_ref.shape[1], 2 * rank))
    for copy in copies:
        copy.wait()
    parts = []
    for l in range(leaves):
        rows = []
        for j in range(0, far_share, 2):
            s0 = far_sources[l, owner * far_share + j]
            s1 = far_sources[l, owner * far_share + j + 1]
            first = table[((s0 ^ mask) >> 1) + (s0 & 1) * half]
            second = table[((s1 ^ mask) >> 1) + half - (s1 & 1) * half]
            rows.append(jnp.where(low, first, second))
        parts.append(
            dot(jnp.concatenate(rows, axis=-1), far_blocks_ref[l].reshape(far_share * rank, rank))
        )
    for l in range(leaves):
        if REACH <= l < leaves - REACH:
            close = near_ref[l - REACH]
        else:
            rows = [
                panels[i] for i in near_rows(near_sources, owner, z, l, leaves, near_share)
            ]
            close = dot(
                jnp.concatenate(rows, axis=-1),
                near_blocks_ref[l].reshape(near_share * panel, panel),
            )
        total_ref[l] = close + dot(parts[l].astype(BF), basis_ref[l])


def down_kernel(total_ref, down_ref, first_ref, second_ref, weight_ref, send_ref, keep_ref):
    leaves, vectors, panel = total_ref.shape
    c = lax.axis_index("lvl")
    own, first, second = (r[...].astype(F32) for r in (down_ref, first_ref, second_ref))
    sources = jnp.concatenate(
        [jnp.where(c == 0, own, first), jnp.where(c == 0, first, second)], axis=-1
    ).astype(BF)
    rows = vectors // 4
    for l in range(leaves):
        part = total_ref[l] + dot(sources, weight_ref[l].reshape(sources.shape[1], panel))
        lanes = slice(l * panel, (l + 1) * panel)
        for w in range(2):
            even = part[2 * w * rows:(2 * w + 1) * rows]
            odd = part[(2 * w + 1) * rows:(2 * w + 2) * rows]
            keep_ref[w, :, lanes] = jnp.where(c == 0, even, odd)
            send_ref[w, :, lanes] = jnp.where(c == 0, odd, even).astype(BF)


def merge_kernel(keep_ref, got_ref, send_ref, rest_ref):
    v = lax.axis_index("vec")
    send_ref[...] = (keep_ref[1 - v] + got_ref[1 - v].astype(F32)).astype(BF)
    rest_ref[...] = keep_ref[v] + got_ref[v].astype(F32)


def in_hbm(*arrays):
    return [pltpu.with_memory_space_constraint(x, pltpu.HBM) for x in arrays]


def swap(x, route):
    axes = ("leaf", "vec", "lvl")
    zs, vs, cs = (lax.axis_size(a) for a in axes)
    pairs = []
    for z in range(zs):
        for v in range(vs):
            for c in range(cs):
                target = route(z, v, c)
                if target is not None:
                    tz, tv, tc = target
                    pairs.append(((z * vs + v) * cs + c, (tz * vs + tv) * cs + tc))
    return lax.ppermute(x, axes, pairs)


def on_device_paired(
    adjoint_in,
    row_basis,
    col_basis,
    row_transfer,
    col_transfer,
    parents,
    far_sources,
    far_blocks,
    coarse_sources,
    coarse_blocks,
    near_sources,
    near_blocks,
):
    vectors = adjoint_in.shape[0]
    leaves, rank, panel = row_basis.shape
    clusters = coarse_sources.shape[0] * 4
    width = leaves * panel
    params = pltpu.CompilerParams(vmem_limit_bytes=LIMIT)
    wide = 2 * rank
    messages = leaves // 2 + clusters // 2
    edges = REACH * panel // wide

    def other_core(z, v, c):
        return z, v, 1 - c

    def other_chip(z, v, c):
        return z, 1 - v, c

    msg, short, packed = pl.pallas_call(
        up_kernel,
        out_shape=(
            jax.ShapeDtypeStruct((messages + edges, vectors, wide), BF),
            jax.ShapeDtypeStruct((messages, vectors, wide), BF),
            jax.ShapeDtypeStruct((coarse_blocks.shape[1], rank, wide), BF),
        ),
        in_specs=[HBM] * 5,
        out_specs=(VMEM,) * 3,
        scratch_shapes=[
            pltpu.VMEM(adjoint_in.shape, BF),
            pltpu.VMEM(row_basis.shape, BF),
            pltpu.VMEM(row_transfer.shape, BF),
            pltpu.SMEM(parents.shape, jnp.int32),
            pltpu.VMEM(coarse_blocks.shape, BF),
            pltpu.VMEM((clusters, vectors, rank), F32),
            pltpu.SemaphoreType.DMA((5,)),
        ],
        compiler_params=params,
        cost_estimate=cost(1.5),
        name="up",
    )(*in_hbm(adjoint_in, row_basis, row_transfer, parents, coarse_blocks))
    a = swap(msg, lambda z, v, c: (z ^ (3 if c else 1), v, c))
    b = swap(short, lambda z, v, c: (z ^ 2, v, c) if c else None)
    p_lvl = swap(packed, other_core)
    near, weight = pl.pallas_call(
        prep_kernel,
        out_shape=(
            jax.ShapeDtypeStruct((leaves - 2 * REACH, vectors, panel), F32),
            jax.ShapeDtypeStruct((leaves, 4, rank, panel), BF),
        ),
        in_specs=[HBM] * 2 + [VMEM] * 4,
        out_specs=(VMEM,) * 2,
        scratch_shapes=[
            pltpu.SMEM(near_sources.shape, jnp.int32),
            pltpu.SMEM(parents.shape, jnp.int32),
            pltpu.VMEM((leaves + 2 * REACH, vectors, panel), BF),
            pltpu.SemaphoreType.DMA((2,)),
        ],
        compiler_params=params,
        cost_estimate=cost(1.5),
        name="prep",
    )(
        *in_hbm(near_sources, parents), adjoint_in, *in_hbm(near_blocks), col_transfer, col_basis
    )
    mix = pl.pallas_call(
        mix_kernel,
        out_shape=jax.ShapeDtypeStruct((clusters, rank, wide), BF),
        in_specs=[HBM] + [VMEM] * 2,
        out_specs=VMEM,
        scratch_shapes=[
            pltpu.SMEM(coarse_sources.shape, jnp.int32),
            pltpu.VMEM((clusters, rank, wide), F32),
            pltpu.SemaphoreType.DMA(()),
        ],
        compiler_params=params,
        cost_estimate=cost(0.1),
        name="mix",
    )(*in_hbm(coarse_sources), packed, p_lvl)
    a, near, weight, mix = lax.optimization_barrier((a, near, weight, mix))
    la = swap(a, other_core)
    lb = swap(b, other_core)

    def coarse(*pieces):
        return pl.pallas_call(
            coarse_kernel,
            out_shape=jax.ShapeDtypeStruct((vectors, wide), BF),
            in_specs=[VMEM] * (len(pieces) + 1),
            out_specs=VMEM,
            compiler_params=params,
            cost_estimate=cost(0.2),
            name="coarse",
        )(*pieces, mix)

    down = coarse(msg, a, la, b, lb)
    first = swap(down, lambda z, v, c: (z ^ (1 if c else 3), v, c))
    second = swap(down, lambda z, v, c: (z ^ 2, v, c) if c else None)
    total = pl.pallas_call(
        local_kernel,
        out_shape=jax.ShapeDtypeStruct((leaves, vectors, panel), F32),
        in_specs=[HBM] * 2 + [VMEM] * 10,
        out_specs=VMEM,
        scratch_shapes=[
            pltpu.SMEM(near_sources.shape, jnp.int32),
            pltpu.SMEM(far_sources.shape, jnp.int32),
            pltpu.VMEM((leaves + 2 * REACH, vectors, panel), BF),
            pltpu.VMEM((4 * leaves, vectors, wide), BF),
            pltpu.SemaphoreType.DMA((2,)),
        ],
        compiler_params=params,
        cost_estimate=cost(4.0),
        name="local",
    )(
        near_sources, far_sources,
        msg, a, b, la, lb, adjoint_in, near_blocks, far_blocks, col_basis, near,
    )
    rows = vectors // 4
    send, keep = pl.pallas_call(
        down_kernel,
        out_shape=(
            jax.ShapeDtypeStruct((2, rows, width), BF),
            jax.ShapeDtypeStruct((2, rows, width), F32),
        ),
        in_specs=[VMEM] * 5,
        out_specs=(VMEM,) * 2,
        compiler_params=params,
        cost_estimate=cost(1.0),
        name="down",
    )(total, down, first, second, weight)
    came = swap(send, other_core)
    send, rest = pl.pallas_call(
        merge_kernel,
        out_shape=(
            jax.ShapeDtypeStruct((rows, width), BF),
            jax.ShapeDtypeStruct((rows, width), F32),
        ),
        in_specs=[VMEM] * 2,
        out_specs=(VMEM,) * 2,
        compiler_params=params,
        cost_estimate=cost(0.6),
        name="merge",
    )(keep, came)
    came = swap(send, other_chip)
    return (rest + came.astype(F32)).astype(BF)


def solution(mesh):
    in_specs = (
        P("groups", "leaf"),
        P(("groups", "leaf"), None, None),
        P(("groups", "leaf"), None, None),
        P(("groups", "leaf"), None, None),
        P(("groups", "leaf"), None, None),
        P(("groups", "leaf")),
        P(("groups", "leaf"), None),
        P(("groups", "leaf"), ("vec", "lvl"), None, None),
        P(("groups", "leaf"), None),
        P(("groups", "leaf"), ("vec", "lvl"), None, None),
        P(("groups", "leaf"), None),
        P(("groups", "leaf"), ("vec", "lvl"), None, None),
    )
    out_specs = P(("groups", "vec", "lvl"), "leaf")
    sizes = tuple(mesh.shape[a] for a in ("leaf", "vec", "lvl"))
    body = on_device_paired if sizes == (4, 2, 2) else on_device_general
    return jax.shard_map(
        body, mesh=mesh, in_specs=in_specs, out_specs=out_specs, check_vma=False
    )
```
